32 devices in a mesh: section: 2 (over y), tensor: 4 (over z), fsdp: 4 (over x, core).
Axes of the slice: x: 2, y: 2, z: 4, core: 2. Of those that a mesh axis runs over, the one named last changes fastest.
Arguments:
- images: bfloat16 [2, 4, 729, 1152], P(None, 'fsdp'), may hold values from -6 to 6
- cotangent: bfloat16 [2, 4, 729, 1152], P(None, 'fsdp'), may hold values from -6 to 6
- qkv_weight: bfloat16 [2, 3, 1152, 1152], P('section', None, 'fsdp', 'tensor'), may hold values from -1 to 1
- qv_bias: bfloat16 [2, 2, 1152], P('section', None, 'tensor'), may hold values from -3 to 3
- out_weight: bfloat16 [2, 1152, 1152], P('section', 'tensor', 'fsdp'), may hold values from -0.75 to 0.75
- up_weight: bfloat16 [2, 1152, 4304], P('section', 'fsdp', 'tensor'), may hold values from -0.1875 to 0.1875
- up_bias: bfloat16 [2, 4304], P('section', 'tensor'), may hold values from -3 to 3
- down_weight: bfloat16 [2, 4304, 1152], P('section', 'tensor', 'fsdp'), may hold values from -0.09375 to 0.09375
- gains: bfloat16 [2, 2, 1152], P('section', None, 'fsdp'), may hold values from 0.099609375 to 1.8984375
- shifts: bfloat16 [2, 4, 1152], P('section', None, 'fsdp'), may hold values from -3 to 3
Outputs:
- section_outputs: bfloat16 [2, 2, 4, 729, 1152], P('section', None, 'fsdp')
- input_grads: bfloat16 [2, 2, 4, 729, 1152], P('section', None, 'fsdp')
- grad_qkv: float32 [2, 3, 1152, 1152], P('section', None, 'fsdp', 'tensor')
- grad_qv_bias: float32 [2, 2, 1152], P('section', None, 'tensor')
- grad_out: float32 [2, 1152, 1152], P('section', 'tensor', 'fsdp')
- grad_up: float32 [2, 1152, 4304], P('section', 'fsdp', 'tensor')
- grad_up_bias: float32 [2, 4304], P('section', 'tensor')
- grad_down: float32 [2, 4304, 1152], P('section', 'tensor', 'fsdp')
- grad_gains: float32 [2, 2, 1152], P('section', None, 'fsdp')
- grad_shifts: float32 [2, 4, 1152], P('section', None, 'fsdp')
The draws below stay inside these ranges and needn't reach their ends.
All inputs are finite; a program needn't handle non-finite values.
Results may differ from the reference program's by a relative error of at most 0.013.
Values may be sent and summed in bfloat16 or wider, within the bound.
A program may use at most 256 MiB of HBM per device.

```python
import jax
import jax.numpy as jnp
from jax import lax

D = 1152
H = 16
HD = 72
FF = 4304
SEQ = 729
MICRO = 2
IMAGES = 4


def draw_qkv_weight(key, part):
    base = jax.random.normal(key, (2, 3, D, D), jnp.float32) * D ** (-0.5)
    return jnp.clip(base, -1.0, 1.0).astype(jnp.bfloat16)


def steps_of(key, extent, pieces, smallest, top_value):
    def one(position, blocks):
        heights = jax.random.uniform(jax.random.fold_in(jax.random.fold_in(key, 6), position), (blocks,), jnp.float32, smallest / len(pieces), top_value / len(pieces))
        return jnp.repeat(jnp.exp(heights), extent[position] // blocks).reshape((-1,) + (1,) * (len(extent) - position - 1))

    level = one(*pieces[0])
    for cut in pieces[1:]:
        level = level * one(*cut)
    return level


def normal_values(rng, shape, deviation, reach, split=(), dtype=jnp.bfloat16):
    drawn = deviation * jax.random.normal(rng, shape, jnp.float32)
    if split:
        drawn = drawn * steps_of(rng, shape, split, -0.22, 0.18)
    return jnp.clip(drawn, -reach, reach).astype(dtype)


def setup_inputs(seed: int = 0) -> dict:
    keys = jax.random.split(jax.random.key(seed), 11)
    images = normal_values(keys[0], (MICRO, IMAGES, SEQ, D), 1.0, 6.0, ((1, 4),))
    cotangent = normal_values(keys[1], (MICRO, IMAGES, SEQ, D), 1.0, 6.0, ((1, 4),))
    qkv_weight = draw_qkv_weight(jax.random.fold_in(keys[10], 71), 0)
    qv_bias = normal_values(keys[3], (2, 2, D), 0.5, 3.0, ((0, 2), (2, 4)))
    out_weight = normal_values(keys[4], (2, D, D), (D // 16) ** -0.5, 0.75, ((0, 2), (1, 4), (2, 4)))
    up_weight = normal_values(keys[5], (2, D, FF), D ** -0.5, 0.1875, ((0, 2), (1, 4), (2, 4)))
    up_bias = normal_values(keys[6], (2, FF), 0.5, 3.0, ((0, 2), (1, 4)))
    down_weight = normal_values(keys[7], (2, FF, D), FF ** -0.5, 0.09375, ((0, 2), (1, 4), (2, 4)))
    gains = jnp.clip(1.0 + 0.18 * jax.random.normal(keys[8], (2, 2, D), jnp.float32), 0.099609375, 1.8984375).astype(jnp.bfloat16)
    shifts = normal_values(keys[9], (2, 4, D), 0.5, 3.0, ((0, 2), (2, 4)))
    return {"images": images, "cotangent": cotangent, "qkv_weight": qkv_weight, "qv_bias": qv_bias, "out_weight": out_weight, "up_weight": up_weight, "up_bias": up_bias, "down_weight": down_weight, "gains": gains, "shifts": shifts}


@jax.custom_vjp
def low(v):
    return lax.optimization_barrier(v.astype(jnp.bfloat16)).astype(jnp.float32)

@jax.custom_vjp
def low_back(v):
    return v

def low_keep(v):
    return (low(v), None)

def low_pass(kept, grad):
    return (grad,)

def back_keep(v):
    return (v, None)

def back_low(kept, grad):
    return (low(grad),)
low.defvjp(low_keep, low_pass)
low_back.defvjp(back_keep, back_low)
NORM_EPS = 1e-06
GELU_ROOT = 0.7978845608028654
GELU_CUBIC = 0.044715

def matmul(left, right):
    return jnp.dot(left, right, precision=lax.Precision.HIGHEST)

def layer_norm(token_rows, gain, shift):
    mean_row = lax.optimization_barrier(jnp.mean(token_rows, axis=-1, keepdims=True))
    centred = token_rows - mean_row
    variance = lax.optimization_barrier(jnp.mean(centred * centred, axis=-1, keepdims=True))
    return centred * lax.rsqrt(variance + NORM_EPS) * gain + shift

def gelu_tanh(value):
    return 0.5 * value * (1.0 + jnp.tanh(GELU_ROOT * (value + GELU_CUBIC * value * value * value)))

def attend(triple):
    queries, key_rows, values = triple
    scores = jnp.einsum('qhd,khd->hqk', queries, key_rows, precision=lax.Precision.HIGHEST) * HD ** (-0.5)
    scores = low_back(scores)
    row_max = lax.optimization_barrier(jnp.max(scores, axis=-1, keepdims=True))
    exp_scores = jnp.exp(scores - row_max)
    attn_probs = low(exp_scores / lax.optimization_barrier(jnp.sum(exp_scores, axis=-1, keepdims=True)))
    return jnp.einsum('hqk,khd->qhd', attn_probs, values, precision=lax.Precision.HIGHEST)

def layer(block_rows, qkv_weight, qv_bias, out_weight, up_weight, up_bias, down_weight, gains, shifts):
    count = block_rows.shape[0]
    token_rows = block_rows.reshape(-1, D)
    normed_one = low(layer_norm(token_rows, gains[0], shifts[0]))
    queries = low(low_back(matmul(normed_one, qkv_weight[0]) + qv_bias[0]))
    key_rows = low(low_back(matmul(normed_one, qkv_weight[1])))
    values = low(low_back(matmul(normed_one, qkv_weight[2]) + qv_bias[1]))
    head_shape = (count, SEQ, H, HD)
    context = lax.map(jax.checkpoint(attend), (queries.reshape(head_shape), key_rows.reshape(head_shape), values.reshape(head_shape)))
    context = low(low_back(context.reshape(-1, D)))
    attn_part = low_back(matmul(context, out_weight) + shifts[1])
    hidden = token_rows + attn_part
    normed_two = low(layer_norm(hidden, gains[1], shifts[2]))
    pre_act = low_back(matmul(normed_two, up_weight) + up_bias)
    active = low(gelu_tanh(pre_act))
    mlp_part = low_back(matmul(active, down_weight) + shifts[3])
    return (hidden + mlp_part).reshape(count, SEQ, D)

def reference(images, cotangent, qkv_weight, qv_bias, out_weight, up_weight, up_bias, down_weight, gains, shifts):
    arrays = [item.astype(jnp.float32) for item in (qkv_weight, qv_bias, out_weight, up_weight, up_bias, down_weight, gains, shifts)]
    first = [item[0] for item in arrays]
    second = [item[1] for item in arrays]
    total = MICRO * IMAGES
    inputs = images.reshape(total, SEQ, D).astype(jnp.float32)
    output_one, back_one = jax.vjp(layer, inputs, *first)
    low_one = output_one.astype(jnp.bfloat16)
    output_two, back_two = jax.vjp(layer, low_one.astype(jnp.float32), *second)
    grads_two = back_two(cotangent.reshape(total, SEQ, D).astype(jnp.float32))
    sent_back = grads_two[0].astype(jnp.bfloat16)
    grads_one = back_one(sent_back.astype(jnp.float32))
    shape5 = (2, MICRO, IMAGES, SEQ, D)
    section_outputs = jnp.stack([low_one, output_two.astype(jnp.bfloat16)]).reshape(shape5)
    input_grads = jnp.stack([grads_one[0].astype(jnp.bfloat16), sent_back]).reshape(shape5)
    stacked = [jnp.stack([grads_one[place], grads_two[place]]) for place in range(1, 9)]
    return (section_outputs, input_grads, stacked[0], stacked[1], stacked[2], stacked[3], stacked[4], stacked[5], stacked[6], stacked[7])
```

```python
import functools

import jax
import jax.numpy as jnp
from jax import lax
from jax.experimental import pallas as pl
from jax.experimental.pallas import tpu as pltpu
from jax.sharding import PartitionSpec as P

HD = 72


NORM_EPS = 1e-06
GELU_ROOT = 0.7978845608028654
GELU_CUBIC = 0.044715
F32 = jnp.float32
BF16 = jnp.bfloat16


MESH = pl.DeviceIdType.MESH
TILE = 16


def greet(me, count):
    barrier = pltpu.get_barrier_semaphore()
    for there, other in ((me > 0, me - 1), (me < count - 1, me + 1)):
        @pl.when(there)
        def _():
            pl.semaphore_signal(barrier, inc=1, device_id={"tensor": other}, device_id_type=MESH)
    peers = (me > 0).astype(jnp.int32) + (me < count - 1).astype(jnp.int32)
    pl.semaphore_wait(barrier, peers)

def line_sum_kernel(count, rows, lag, x_ref, o_ref, come, gone, red_send, red_recv, out_send, out_recv):
    me = lax.axis_index("tensor")
    greet(me, count)
    pieces = x_ref.shape[0] // rows

    def span(piece):
        return pl.ds(pl.multiple_of(piece * rows, rows), rows)

    def send(piece, source, target, step, out):
        sems = (out_send, out_recv) if out else (red_send, red_recv)
        return pltpu.make_async_remote_copy(
            src_ref=source.at[span(piece)],
            dst_ref=target.at[span(piece)],
            send_sem=sems[0].at[piece],
            recv_sem=sems[1].at[piece],
            device_id={"tensor": me + step},
            device_id_type=MESH,
        )

    def place(step):
        return me if step > 0 else count - 1 - me

    def reduce_step(index, step):
        piece = 2 * index + (step < 0)
        ok = (index >= 0) & (piece < pieces)
        pos = place(step)

        @pl.when(ok & (pos == 0))
        def _():
            send(piece, x_ref, come, step, False).start()

        def add():
            send(piece, come, come, step, False).wait_recv()
            return (x_ref[span(piece), :].astype(F32) + come[span(piece), :].astype(F32)).astype(BF16)

        @pl.when(ok & (pos > 0) & (pos < count - 1))
        def _():
            gone[span(piece), :] = add()
            send(piece, gone, come, step, False).start()

        @pl.when(ok & (pos == count - 1))
        def _():
            o_ref[span(piece), :] = add()
            send(piece, o_ref, o_ref, -step, True).start()

    def out_step(index, step):
        piece = 2 * index + (step < 0)
        ok = (index >= 0) & (piece < pieces)
        pos = place(step)

        @pl.when(ok & (pos < count - 1))
        def _():
            send(piece, o_ref, o_ref, -step, True).wait_recv()

        @pl.when(ok & (pos > 0) & (pos < count - 1))
        def _():
            send(piece, o_ref, o_ref, -step, True).start()

    pairs = (pieces + 1) // 2

    def turn(s, _):
        for step in (1, -1):
            reduce_step(s - lag * place(step), step)
        for step in (1, -1):
            out_step(s - lag * (count - 1) - lag * (count - 1 - place(step)), step)
        return 0

    lax.fori_loop(0, pairs + 2 * lag * (count - 1), turn, 0)

    def end_steps(i, _):
        for step in (1, -1):
            piece = 2 * i + (step < 0)
            pos = place(step)

            @pl.when((piece < pieces) & (pos < count - 1))
            def _():
                send(piece, x_ref, come, step, False).wait_send()

            @pl.when((piece < pieces) & (pos > 0))
            def _():
                send(piece, o_ref, o_ref, -step, True).wait_send()
        return 0

    lax.fori_loop(0, pairs, end_steps, 0)


def line_sum(x, cid, rows=16, lag=4):
    count = lax.axis_size("tensor")
    pieces = x.shape[0] // rows
    return pl.pallas_call(
        functools.partial(line_sum_kernel, count, rows, lag),
        out_shape=jax.ShapeDtypeStruct(x.shape, BF16),
        in_specs=[pl.BlockSpec(memory_space=pltpu.VMEM)],
        out_specs=pl.BlockSpec(memory_space=pltpu.VMEM),
        scratch_shapes=[
            pltpu.VMEM(x.shape, BF16),
            pltpu.VMEM(x.shape, BF16),
        ] + [pltpu.SemaphoreType.DMA((pieces,))] * 4,
        compiler_params=pltpu.CompilerParams(collective_id=cid, has_side_effects=True),
        name="line_sum",
        cost_estimate=pl.CostEstimate(flops=0, bytes_accessed=120_000_000, transcendentals=0),
    )(x)


def tensor_sum(value):
    return line_sum(value.astype(BF16), 0).astype(F32)


def gelu_value(value):
    return 0.5 * value * (1.0 + jnp.tanh(GELU_ROOT * (value + GELU_CUBIC * value * value * value)))


def gelu_slope(value):
    inner = jnp.tanh(GELU_ROOT * (value + GELU_CUBIC * value * value * value))
    return 0.5 * (1.0 + inner) + 0.5 * value * (1.0 - inner * inner) * GELU_ROOT * (
        1.0 + 3.0 * GELU_CUBIC * value * value
    )


def norm_forward(token_rows, gain, shift):
    mean_row = jnp.mean(token_rows, axis=-1, keepdims=True)
    centred = token_rows - mean_row
    inverse = lax.rsqrt(jnp.mean(centred * centred, axis=-1, keepdims=True) + NORM_EPS)
    normed = centred * inverse
    return (normed * gain + shift, normed, inverse)


def norm_backward(grad_normed, normed, inverse, gain):
    scaled = grad_normed * gain
    inner = (
        scaled
        - jnp.mean(scaled, axis=-1, keepdims=True)
        - normed * jnp.mean(scaled * normed, axis=-1, keepdims=True)
    )
    return (inverse * inner, jnp.sum(grad_normed * normed, axis=0), jnp.sum(grad_normed, axis=0))


def dot_nn(left, right):
    return jnp.dot(left, right, preferred_element_type=F32)


def dot_nt(left, right):
    return lax.dot_general(left, right, (((1,), (1,)), ((), ())), preferred_element_type=F32)


def dot_tn(left, right):
    return lax.dot_general(left, right, (((0,), (0,)), ((), ())), preferred_element_type=F32)


def layer_forward(inputs, weights, qv_bias, up_bias, gains, shifts, cuts, real):
    qkv, out_t, up, down_t = weights
    width = qkv.shape[1] // 3
    heads = width // HD
    scale = HD ** (-0.5)
    seq_len = cuts[-1][1]
    normed_one = []
    parts = []
    for part in inputs:
        normed = norm_forward(part.astype(F32), gains[0], shifts[0])[0].astype(BF16)
        normed_one.append(normed)
        parts.append(dot_nn(normed, qkv))
    normed_one = jnp.concatenate(normed_one)
    projected = jnp.concatenate(parts)
    queries = (projected[:, :width] + qv_bias[0]).astype(BF16).reshape(seq_len, heads, HD)
    key_rows = projected[:, width : 2 * width].astype(BF16).reshape(seq_len, heads, HD)
    values = (projected[:, 2 * width :] + qv_bias[1]).astype(BF16).reshape(seq_len, heads, HD)
    context, hidden, normed_two, pre_act, active, outputs, log_total = [], [], [], [], [], [], []
    for (first, last), part in zip(cuts, inputs):
        scores = (
            jnp.einsum("qhd,khd->hqk", queries[first:last], key_rows, preferred_element_type=F32)
            * scale
        )
        scores = jnp.where(lax.broadcasted_iota(jnp.int32, scores.shape, 2) < real, scores, -1e30)
        row_max = jnp.max(scores, axis=-1, keepdims=True)
        exp_scores = jnp.exp(scores - row_max)
        row_total = jnp.sum(exp_scores, axis=-1, keepdims=True)
        probs = (exp_scores / row_total).astype(BF16)
        log_total.append(row_max + jnp.log(row_total))
        mixed = jnp.einsum("hqk,khd->qhd", probs, values, preferred_element_type=F32)
        context.append(mixed.astype(BF16).reshape(last - first, width))
        attn_term = tensor_sum(dot_nt(context[-1], out_t))
        hidden.append(part.astype(F32) + attn_term + shifts[1])
    for rows in hidden:
        normed = norm_forward(rows, gains[1], shifts[2])[0].astype(BF16)
        normed_two.append(normed)
        pre_act.append(dot_nn(normed, up) + up_bias)
        active.append(gelu_value(pre_act[-1]).astype(BF16))
        mlp_term = tensor_sum(dot_nt(active[-1], down_t))
        outputs.append((rows + mlp_term + shifts[3]).astype(BF16))
    stored = (
        inputs,
        normed_one,
        queries,
        key_rows,
        values,
        log_total,
        context,
        hidden,
        normed_two,
        pre_act,
        active,
    )
    return outputs, stored


def layer_backward(grads, stored, weights, gains, shifts, cuts, real):
    qkv, out_t, up, down_t = weights
    (
        inputs,
        normed_one,
        queries,
        key_rows,
        values,
        log_total,
        context,
        hidden,
        normed_two,
        pre_act,
        active,
    ) = stored
    width = qkv.shape[1] // 3
    scale = HD ** (-0.5)
    grad_mix = [part.astype(BF16) for part in grads]
    grad_pre = []
    two_terms = []
    for part, pre in zip(grad_mix, pre_act):
        grad_active = dot_nn(part, down_t)
        grad_pre.append((grad_active * gelu_slope(pre)).astype(BF16))
        two_terms.append(tensor_sum(dot_nt(grad_pre[-1], up)))
    mix_all = jnp.concatenate(grad_mix)
    pre_all = jnp.concatenate(grad_pre)
    grad_down = dot_tn(mix_all, jnp.concatenate(active))
    grad_up = dot_tn(jnp.concatenate(normed_two), pre_all)
    up_bias_grad = jnp.sum(pre_all.astype(F32), axis=0)
    mix_shift = jnp.sum(mix_all.astype(F32), axis=0)
    grad_hidden, grad_attn, gain_two, shift_two, attn_shift = [], [], 0.0, 0.0, 0.0
    grad_q = []
    grad_k = 0.0
    grad_v = 0.0
    for (first, last), part, two, rows, logs in zip(cuts, grads, two_terms, hidden, log_total):
        normed, inverse = norm_forward(rows, gains[1], shifts[2])[1:]
        moved, gain_part, shift_part = norm_backward(two, normed, inverse, gains[1])
        gain_two += gain_part
        shift_two += shift_part
        grad_hidden.append(part.astype(F32) + moved)
        grad_attn.append(grad_hidden[-1].astype(BF16))
        attn_shift += jnp.sum(grad_attn[-1].astype(F32), axis=0)
        grad_context = dot_nn(grad_attn[-1], out_t).astype(BF16).reshape(last - first, -1, HD)
        scores = (
            jnp.einsum("qhd,khd->hqk", queries[first:last], key_rows, preferred_element_type=F32)
            * scale
        )
        probs = jnp.exp(scores - logs)
        probs = jnp.where(lax.broadcasted_iota(jnp.int32, scores.shape, 2) < real, probs, 0.0)
        mixed = jnp.einsum("qhd,khd->hqk", grad_context, values, preferred_element_type=F32)
        row_delta = jnp.sum(mixed * probs, axis=-1, keepdims=True)
        grad_scores = (probs * (mixed - row_delta)).astype(BF16)
        grad_v += jnp.einsum("hqk,qhd->khd", probs.astype(BF16), grad_context, preferred_element_type=F32)
        grad_q.append(
            (jnp.einsum("hqk,khd->qhd", grad_scores, key_rows, preferred_element_type=F32) * scale).astype(BF16)
        )
        grad_k += jnp.einsum("hqk,qhd->khd", grad_scores, queries[first:last], preferred_element_type=F32)
    grad_proj = jnp.concatenate(
        [
            jnp.concatenate(grad_q).reshape(-1, width),
            (grad_k * scale).astype(BF16).reshape(-1, width),
            grad_v.astype(BF16).reshape(-1, width),
        ],
        axis=1,
    )
    context_all = jnp.concatenate(context)
    attn_all = jnp.concatenate(grad_attn)
    grad_out = dot_tn(attn_all, context_all)
    grad_qkv = dot_tn(normed_one, grad_proj)
    bias_sums = jnp.sum(grad_proj.astype(F32), axis=0)
    grad_inputs = []
    gain_one, shift_one = 0.0, 0.0
    one_terms = [tensor_sum(dot_nt(grad_proj[first:last], qkv)) for first, last in cuts]
    for one, part, rows in zip(one_terms, inputs, grad_hidden):
        normed, inverse = norm_forward(part.astype(F32), gains[0], shifts[0])[1:]
        moved, gain_part, shift_part = norm_backward(one, normed, inverse, gains[0])
        gain_one += gain_part
        shift_one += shift_part
        grad_inputs.append((rows + moved).astype(BF16))
    gain_grads = [gain_one, gain_two, shift_one, attn_shift, shift_two, mix_shift]
    bias_grads = jnp.concatenate([bias_sums[:width], bias_sums[2 * width :], up_bias_grad])
    return grad_inputs, (grad_qkv, grad_out, grad_up, grad_down), (jnp.concatenate(gain_grads), bias_grads)


def per_device(
    images,
    cotangent,
    qkv_weight,
    qv_bias,
    out_weight,
    up_weight,
    up_bias,
    down_weight,
    gains,
    shifts,
):
    image_count, seq_len, model_width = images.shape[1:]
    rows_here = qkv_weight.shape[2]
    width = qkv_weight.shape[3]
    units = up_weight.shape[2]
    section = lax.axis_index("section")
    fsdp = lax.axis_index("fsdp")
    is_first = section == 0
    every = ("section", "fsdp")
    padded = -(-seq_len // TILE) * TILE
    cuts = [(0, padded)]

    def gathered(piece):
        whole = lax.all_gather(piece, every, axis=0, tiled=True)
        return whole.reshape(2, -1, piece.shape[1])

    qkv = gathered(qkv_weight[0].transpose(1, 0, 2).reshape(rows_here, 3 * width))
    out_t = gathered(out_weight[0].T)
    up = gathered(up_weight[0])
    down_t = gathered(down_weight[0].T)
    scales = lax.all_gather(
        jnp.concatenate([gains[0], shifts[0]]), every, axis=0, tiled=False
    )
    scales = scales.reshape(2, -1, 6, rows_here).transpose(0, 2, 1, 3).reshape(2, 6, model_width)
    scales = scales.astype(F32)
    biases = lax.all_gather(
        jnp.concatenate([qv_bias.reshape(-1), up_bias.reshape(-1)]), "section", axis=0
    ).astype(F32)

    def padded_rows(array):
        rows = lax.dynamic_index_in_dim(array, section, 0, keepdims=False)[0]
        return jnp.pad(rows, ((0, padded - seq_len), (0, 0)))

    def layer_args(index):
        return (qkv[index], out_t[index], up[index], down_t[index])

    own = padded_rows(images)
    own_grad = padded_rows(cotangent)
    rows = [own[first:last] for first, last in cuts]
    outputs, stored = [], []
    for index in range(2):
        qv = biases[index, : 2 * width].reshape(2, width)
        rows, kept = layer_forward(
            rows, layer_args(index), qv, biases[index, 2 * width :], scales[index, :2], scales[index, 2:], cuts, seq_len
        )
        outputs.append(jnp.concatenate(rows))
        stored.append(kept)

    def swapped(pair):
        pair = [item[:seq_len] for item in pair]
        mine = jnp.where(is_first, pair[0], pair[1])
        other = lax.ppermute(jnp.where(is_first, pair[1], pair[0]), "section", [(0, 1), (1, 0)])
        return jnp.where(
            is_first, jnp.stack([mine, other]), jnp.stack([other, mine])
        )[None, :, None]

    section_outputs = swapped(outputs)
    grads = [own_grad[first:last] for first, last in cuts]
    input_grads = [None, None]
    weight_grads = [None, None]
    small = [None, None]
    for index in (1, 0):
        grads, weight_grads[index], small[index] = layer_backward(
            grads, stored[index], layer_args(index), scales[index, :2], scales[index, 2:], cuts, seq_len
        )
        input_grads[index] = jnp.concatenate(grads)
    input_grads = swapped(input_grads)

    def scattered(pair):
        pieces = [
            lax.psum_scatter(item.astype(BF16), "fsdp", scatter_dimension=0, tiled=True) for item in pair
        ]
        mine = jnp.where(is_first, pieces[0], pieces[1])
        other = lax.ppermute(jnp.where(is_first, pieces[1], pieces[0]), "section", [(0, 1), (1, 0)])
        return mine.astype(F32) + other.astype(F32)

    grad_qkv, grad_out, grad_up, grad_down = [
        scattered([weight_grads[0][place], weight_grads[1][place]]) for place in range(4)
    ]
    packed = jnp.stack([jnp.concatenate(small[0]), jnp.concatenate(small[1])])
    packed = lax.psum(packed, every)
    packed = jnp.where(is_first, packed[0], packed[1])
    norm_part = packed[: 6 * model_width].reshape(6, model_width)
    norm_part = lax.dynamic_slice_in_dim(norm_part, fsdp * rows_here, rows_here, 1)
    bias_part = packed[6 * model_width :]
    return (
        section_outputs,
        input_grads,
        grad_qkv.reshape(rows_here, 3, width).transpose(1, 0, 2)[None],
        bias_part[: 2 * width].reshape(1, 2, width),
        grad_out.T[None],
        grad_up[None],
        bias_part[2 * width :][None],
        grad_down.T[None],
        norm_part[:2][None],
        norm_part[2:][None],
    )


def solution(mesh):
    return jax.shard_map(
        per_device,
        mesh=mesh,
        in_specs=(
            P(None, "fsdp", None, None),
            P(None, "fsdp", None, None),
            P("section", None, "fsdp", "tensor"),
            P("section", None, "tensor"),
            P("section", "tensor", "fsdp"),
            P("section", "fsdp", "tensor"),
            P("section", "tensor"),
            P("section", "tensor", "fsdp"),
            P("section", None, "fsdp"),
            P("section", None, "fsdp"),
        ),
        out_specs=(
            P("section", None, "fsdp", None, None),
            P("section", None, "fsdp", None, None),
            P("section", None, "fsdp", "tensor"),
            P("section", None, "tensor"),
            P("section", "tensor", "fsdp"),
            P("section", "fsdp", "tensor"),
            P("section", "tensor"),
            P("section", "tensor", "fsdp"),
            P("section", None, "fsdp"),
            P("section", None, "fsdp"),
        ),
        check_vma=False,
    )
```

```python
import functools

import jax
import jax.numpy as jnp
from jax import lax
from jax.experimental import pallas as pl
from jax.experimental.pallas import tpu as pltpu
from jax.sharding import PartitionSpec as P
from jax.experimental.layout import Layout, with_layout_constraint

HD = 72


NORM_EPS = 1e-06
GELU_ROOT = 0.7978845608028654
GELU_CUBIC = 0.044715
F32 = jnp.float32
BF16 = jnp.bfloat16


MESH = pl.DeviceIdType.MESH
TILE = 16


def greet(me, count, others=()):
    barrier = pltpu.get_barrier_semaphore()
    for there, other in ((me > 0, me - 1), (me < count - 1, me + 1)):
        @pl.when(there)
        def _():
            pl.semaphore_signal(barrier, inc=1, device_id={"tensor": other}, device_id_type=MESH)
    for other in others:
        pl.semaphore_signal(barrier, inc=1, device_id=other, device_id_type=MESH)
    peers = (me > 0).astype(jnp.int32) + (me < count - 1).astype(jnp.int32)
    pl.semaphore_wait(barrier, peers + len(others))


class Line:
    def __init__(self, count, rows, lag, x_ref, o_ref, come, gone, sems):
        self.count, self.rows, self.lag = count, rows, lag
        self.x, self.o, self.come, self.gone = x_ref, o_ref, come, gone
        self.red, self.out = sems[:2], sems[2:]
        self.me = lax.axis_index("tensor")
        self.pieces = x_ref.shape[0] // rows
        self.pairs = (self.pieces + 1) // 2
        self.turns = self.pairs + 2 * lag * (count - 1)

    def span(self, piece):
        return pl.ds(pl.multiple_of(piece * self.rows, self.rows), self.rows)

    def send(self, piece, source, target, step, sems):
        return pltpu.make_async_remote_copy(
            src_ref=source.at[self.span(piece)],
            dst_ref=target.at[self.span(piece)],
            send_sem=sems[0].at[piece],
            recv_sem=sems[1].at[piece],
            device_id={"tensor": self.me + step},
            device_id_type=MESH,
        )

    def place(self, step):
        return self.me if step > 0 else self.count - 1 - self.me

    def reduce_step(self, index, step):
        piece = 2 * index + (step < 0)
        ok = (index >= 0) & (piece < self.pieces)
        pos = self.place(step)
        end = self.count - 1
        span = self.span(piece)

        @pl.when(ok & (pos == 0))
        def _():
            self.send(piece, self.x, self.come, step, self.red).start()

        def add():
            self.send(piece, self.come, self.come, step, self.red).wait_recv()
            return (self.x[span, :].astype(F32) + self.come[span, :].astype(F32)).astype(BF16)

        @pl.when(ok & (pos > 0) & (pos < end))
        def _():
            self.gone[span, :] = add()
            self.send(piece, self.gone, self.come, step, self.red).start()

        @pl.when(ok & (pos == end))
        def _():
            self.o[span, :] = add()
            self.send(piece, self.o, self.o, -step, self.out).start()

    def out_step(self, index, step):
        piece = 2 * index + (step < 0)
        ok = (index >= 0) & (piece < self.pieces)
        pos = self.place(step)

        @pl.when(ok & (pos < self.count - 1))
        def _():
            self.send(piece, self.o, self.o, -step, self.out).wait_recv()

        @pl.when(ok & (pos > 0) & (pos < self.count - 1))
        def _():
            self.send(piece, self.o, self.o, -step, self.out).start()

    def turn(self, s):
        for step in (1, -1):
            self.reduce_step(s - self.lag * self.place(step), step)
        back = self.lag * (self.count - 1)
        for step in (1, -1):
            self.out_step(s - back - self.lag * (self.count - 1 - self.place(step)), step)

    def finish(self):
        def end_steps(i, _):
            for step in (1, -1):
                piece = 2 * i + (step < 0)
                pos = self.place(step)

                @pl.when((piece < self.pieces) & (pos < self.count - 1))
                def _():
                    self.send(piece, self.x, self.come, step, self.red).wait_send()

                @pl.when((piece < self.pieces) & (pos > 0))
                def _():
                    self.send(piece, self.o, self.o, -step, self.out).wait_send()
            return 0

        lax.fori_loop(0, self.pairs, end_steps, 0)

    @staticmethod
    def scratch(x, rows):
        return [pltpu.VMEM(x.shape, BF16)] * 2 + [pltpu.SemaphoreType.DMA((x.shape[0] // rows,))] * 4


class Share:
    def __init__(self, ways, layer, cuts, g_ref, o_ref, bufs):
        self.ways, self.layer, self.cuts = ways, layer, cuts
        self.levels = ways.bit_length() - 1
        self.g, self.o = g_ref, o_ref
        n = self.levels
        self.recv, self.stage = bufs[:n], [None] + list(bufs[n : 2 * n - 1])
        bufs = bufs[2 * n - 1 :]
        self.last_recv, self.last_stage = bufs[:2]
        sems = bufs[2:]
        self.sems = [(sems[2 * j], sems[2 * j + 1]) for j in range(n + 1)]
        self.me = lax.axis_index("fsdp")
        self.owner = lax.axis_index("section") == layer
        self.height = o_ref.shape[0]
        self.rows = self.height // cuts

    def others(self):
        return [{"fsdp": self.flip(j)} for j in range(self.levels)] + [
            {"section": 1 - lax.axis_index("section")}
        ]

    def flip(self, level):
        bit = self.me // (1 << level) % 2
        return self.me + (1 - 2 * bit) * (1 << level)

    def blocks(self, level):
        low = self.flip(level) % (1 << (level + 1))
        return [low + (high << (level + 1)) for high in range(self.ways >> (level + 1))]

    def span(self, piece):
        return pl.ds(pl.multiple_of(piece * self.rows, self.rows), self.rows)

    def own(self, block, piece):
        if len(self.g.shape) == 3:
            return self.g.at[block, self.span(piece)]
        return self.g.at[pl.ds(pl.multiple_of(block * self.height + piece * self.rows, self.rows), self.rows)]

    def copy(self, level, block, piece):
        place = block // (1 << (level + 1))
        return pltpu.make_async_remote_copy(
            src_ref=self.own(block, piece) if level == 0 else self.stage[level].at[place, self.span(piece)],
            dst_ref=self.recv[level].at[place, self.span(piece)],
            send_sem=self.sems[level][0].at[place * self.cuts + piece],
            recv_sem=self.sems[level][1].at[place * self.cuts + piece],
            device_id={"fsdp": self.flip(level)},
            device_id_type=MESH,
        )

    def last_copy(self, piece):
        return pltpu.make_async_remote_copy(
            src_ref=self.last_stage.at[self.span(piece)],
            dst_ref=self.last_recv.at[self.span(piece)],
            send_sem=self.sems[-1][0].at[piece],
            recv_sem=self.sems[-1][1].at[piece],
            device_id={"section": 1 - lax.axis_index("section")},
            device_id_type=MESH,
        )

    def start(self):
        for piece in range(self.cuts):
            for block in self.blocks(0):
                self.copy(0, block, piece).start()

    def total(self, level, block, piece):
        value = self.own(block, piece)[...].astype(F32)
        for j in range(level):
            self.copy(j, block, piece).wait_recv()
            value += self.recv[j][block // (1 << (j + 1)), self.span(piece), :].astype(F32)
        return value

    def step(self, level, piece):
        if level < self.levels:
            for block in self.blocks(level):
                self.stage[level][block // (1 << (level + 1)), self.span(piece), :] = self.total(
                    level, block, piece
                ).astype(BF16)
                self.copy(level, block, piece).start()
        elif level == self.levels:
            value = self.total(level, self.me, piece)
            self.o[self.span(piece), :] = value

            @pl.when(jnp.logical_not(self.owner))
            def _():
                self.last_stage[self.span(piece), :] = value.astype(BF16)
                self.last_copy(piece).start()
        else:

            @pl.when(self.owner)
            def _():
                self.last_copy(piece).wait_recv()
                self.o[self.span(piece), :] += self.last_recv[self.span(piece), :].astype(F32)

    def finish(self):
        for piece in range(self.cuts):
            for level in range(self.levels):
                for block in self.blocks(level):
                    self.copy(level, block, piece).wait_send()

            @pl.when(jnp.logical_not(self.owner))
            def _():
                self.last_copy(piece).wait_send()

    @staticmethod
    def scratch(shape, ways, cuts):
        levels = ways.bit_length() - 1
        rows, width = shape
        counts = [ways >> (j + 1) for j in range(levels)]
        sems = []
        for count in counts + [1]:
            sems += [pltpu.SemaphoreType.DMA((count * cuts,))] * 2
        return (
            [pltpu.VMEM((count, rows, width), BF16) for count in counts + counts[1:]]
            + [pltpu.VMEM((rows, width), BF16)] * 2
            + sems
        )


def line_sum_kernel(count, rows, lag, x_ref, o_ref, come, gone, *sems):
    line = Line(count, rows, lag, x_ref, o_ref, come, gone, sems)
    greet(line.me, count)
    lax.fori_loop(0, line.turns, lambda s, _: (line.turn(s), 0)[1], 0)
    line.finish()


def line_sum(x, cid, rows=16, lag=4):
    count = lax.axis_size("tensor")
    return pl.pallas_call(
        functools.partial(line_sum_kernel, count, rows, lag),
        out_shape=jax.ShapeDtypeStruct(x.shape, BF16),
        in_specs=[pl.BlockSpec(memory_space=pltpu.VMEM)],
        out_specs=pl.BlockSpec(memory_space=pltpu.VMEM),
        scratch_shapes=Line.scratch(x, rows),
        compiler_params=pltpu.CompilerParams(collective_id=cid, has_side_effects=True),
        name="line_sum",
        cost_estimate=pl.CostEstimate(flops=0, bytes_accessed=120_000_000, transcendentals=0),
    )(x)


def line_share_kernel(count, rows, lag, ways, layer, cuts, k, *refs):
    x_ref, g_refs = refs[0], refs[1 : 1 + k]
    o_ref, go_refs = refs[1 + k], refs[2 + k : 2 + 2 * k]
    scratch = refs[2 + 2 * k :]
    line = Line(count, rows, lag, x_ref, o_ref, *scratch[:2], scratch[2:6])
    scratch = scratch[6:]
    each = len(scratch) // k
    shares = [
        Share(ways, layer, cuts, g_refs[i], go_refs[i], scratch[i * each : (i + 1) * each]) for i in range(k)
    ]
    levels = shares[0].levels
    greet(line.me, count, shares[0].others())
    for share in shares:
        share.start()
    steps = []
    for level in range(1, levels + 2):
        first, stride = (4, 1) if level == 1 else (3 + 6 * (level - 1), 5)
        steps += [(first + i * cuts * stride, stride, level, share) for i, share in enumerate(shares)]
    turns = max(line.turns, max(first + stride * (cuts - 1) + 1 for first, stride, _, _ in steps))

    def turn(s, _):
        line.turn(s)
        for first, stride, level, share in steps:
            past = s - first
            piece = past // stride

            @pl.when((past >= 0) & (past % stride == 0) & (piece < cuts))
            def _():
                share.step(level, piece)
        return 0

    lax.fori_loop(0, turns, turn, 0)
    line.finish()
    for share in shares:
        share.finish()


def line_share(x, grads, layer, cid, rows=16, lag=4):
    count, ways = lax.axis_size("tensor"), lax.axis_size("fsdp")
    height = grads[0].shape[0] // ways
    shapes = [(height, g.shape[1]) for g in grads]
    cuts = 3 if height % (3 * TILE) == 0 else 1
    if height % TILE:
        grads = [g.reshape(ways, height, g.shape[1]) for g in grads]
    scratch = Line.scratch(x, rows)
    for shape in shapes:
        scratch += Share.scratch(shape, ways, cuts)
    vmem = pl.BlockSpec(memory_space=pltpu.VMEM)
    return pl.pallas_call(
        functools.partial(
            line_share_kernel, count, rows, lag, ways, layer, cuts, len(grads)
        ),
        out_shape=[jax.ShapeDtypeStruct(x.shape, BF16)]
        + [jax.ShapeDtypeStruct(shape, F32) for shape in shapes],
        in_specs=[vmem] * (1 + len(grads)),
        out_specs=[vmem] * (1 + len(grads)),
        scratch_shapes=scratch,
        compiler_params=pltpu.CompilerParams(
            collective_id=cid, has_side_effects=True, vmem_limit_bytes=56 * 1024 * 1024
        ),
        name="line_share",
        cost_estimate=pl.CostEstimate(flops=0, bytes_accessed=120_000_000, transcendentals=0),
    )(x, *grads)


def tensor_sum(value):
    return line_sum(value.astype(BF16), 0).astype(F32)


def gelu_value(value):
    return 0.5 * value * (1.0 + jnp.tanh(GELU_ROOT * (value + GELU_CUBIC * value * value * value)))


def gelu_slope(value):
    inner = jnp.tanh(GELU_ROOT * (value + GELU_CUBIC * value * value * value))
    return 0.5 * (1.0 + inner) + 0.5 * value * (1.0 - inner * inner) * GELU_ROOT * (
        1.0 + 3.0 * GELU_CUBIC * value * value
    )


def norm_forward(token_rows, gain, shift):
    mean_row = jnp.mean(token_rows, axis=-1, keepdims=True)
    centred = token_rows - mean_row
    inverse = lax.rsqrt(jnp.mean(centred * centred, axis=-1, keepdims=True) + NORM_EPS)
    normed = centred * inverse
    return (normed * gain + shift, normed, inverse)


def norm_backward(grad_normed, normed, inverse, gain):
    scaled = grad_normed * gain
    inner = (
        scaled
        - jnp.mean(scaled, axis=-1, keepdims=True)
        - normed * jnp.mean(scaled * normed, axis=-1, keepdims=True)
    )
    return (inverse * inner, jnp.sum(grad_normed * normed, axis=0), jnp.sum(grad_normed, axis=0))


def dot_nn(left, right):
    return jnp.dot(left, right, preferred_element_type=F32)


def dot_nt(left, right):
    return lax.dot_general(left, right, (((1,), (1,)), ((), ())), preferred_element_type=F32)


def dot_tn(left, right):
    return with_layout_constraint(lax.dot_general(left, right, (((0,), (0,)), ((), ())), preferred_element_type=F32), Layout((0,1)))


def layer_forward(inputs, weights, qv_bias, up_bias, gains, shifts, cuts, real, is_last):
    qkv, out_t, up, down_t = weights
    width = qkv.shape[1] // 3
    heads = width // HD
    scale = HD ** (-0.5)
    seq_len = cuts[-1][1]
    normed_one = []
    parts = []
    for part in inputs:
        normed = norm_forward(part.astype(F32), gains[0], shifts[0])[0].astype(BF16)
        normed_one.append(normed)
        parts.append(dot_nn(normed, qkv))
    normed_one = jnp.concatenate(normed_one)
    projected = jnp.concatenate(parts)
    queries = (projected[:, :width] + qv_bias[0]).astype(BF16).reshape(seq_len, heads, HD)
    key_rows = projected[:, width : 2 * width].astype(BF16).reshape(seq_len, heads, HD)
    values = (projected[:, 2 * width :] + qv_bias[1]).astype(BF16).reshape(seq_len, heads, HD)
    context, hidden, normed_two, pre_act, active, outputs, log_total = [], [], [], [], [], [], []
    for (first, last), part in zip(cuts, inputs):
        scores = (
            jnp.einsum("qhd,khd->hqk", queries[first:last], key_rows, preferred_element_type=F32)
            * scale
        )
        scores = jnp.where(lax.broadcasted_iota(jnp.int32, scores.shape, 2) < real, scores, -1e30)
        row_max = jnp.max(scores, axis=-1, keepdims=True)
        exp_scores = jnp.exp(scores - row_max)
        row_total = jnp.sum(exp_scores, axis=-1, keepdims=True)
        probs = (exp_scores / row_total).astype(BF16)
        log_total.append(row_max + jnp.log(row_total))
        mixed = jnp.einsum("hqk,khd->qhd", probs, values, preferred_element_type=F32)
        context.append(mixed.astype(BF16).reshape(last - first, width))
        attn_term = tensor_sum(dot_nt(context[-1], out_t))
        hidden.append(part.astype(F32) + attn_term + shifts[1])
    for rows in hidden:
        normed = norm_forward(rows, gains[1], shifts[2])[0].astype(BF16)
        normed_two.append(normed)
        pre_act.append(dot_nn(normed, up) + up_bias)
        active.append(gelu_value(pre_act[-1]).astype(BF16))
        mlp_term = dot_nt(active[-1], down_t).astype(BF16)
        if is_last:
            outputs.append(lambda total, rows=rows: (rows + total.astype(F32) + shifts[3]).astype(BF16))
            stored_term = mlp_term
            continue
        outputs.append((rows + line_sum(mlp_term, 0).astype(F32) + shifts[3]).astype(BF16))
        stored_term = None
    stored = (
        inputs,
        normed_one,
        queries,
        key_rows,
        values,
        log_total,
        context,
        hidden,
        normed_two,
        pre_act,
        active,
    )
    return outputs, stored, stored_term


def layer_backward(grads, stored, weights, gains, shifts, cuts, real, layer, extra):
    qkv, out_t, up, down_t = weights
    (
        inputs,
        normed_one,
        queries,
        key_rows,
        values,
        log_total,
        context,
        hidden,
        normed_two,
        pre_act,
        active,
    ) = stored
    width = qkv.shape[1] // 3
    scale = HD ** (-0.5)
    grad_mix = [part.astype(BF16) for part in grads]
    grad_pre = []
    two_terms = []
    for part, pre in zip(grad_mix, pre_act):
        grad_active = dot_nn(part, down_t)
        grad_pre.append((grad_active * gelu_slope(pre)).astype(BF16))
        two_terms.append(dot_nt(grad_pre[-1], up).astype(BF16))
    mix_all = jnp.concatenate(grad_mix)
    pre_all = jnp.concatenate(grad_pre)
    grad_down = dot_tn(mix_all, jnp.concatenate(active))
    grad_up = dot_tn(jnp.concatenate(normed_two), pre_all)
    count = two_terms[0].shape[0]
    two = two_terms[0] if extra is None else jnp.concatenate([two_terms[0], extra])
    two, grad_down, grad_up = line_share(
        two, [grad_down.astype(BF16), grad_up.astype(BF16)], layer, 1 + 2 * layer
    )
    two_terms = [two[:count].astype(F32)]
    extra = two[count:]
    up_bias_grad = jnp.sum(pre_all.astype(F32), axis=0)
    mix_shift = jnp.sum(mix_all.astype(F32), axis=0)
    grad_hidden, grad_attn, gain_two, shift_two, attn_shift = [], [], 0.0, 0.0, 0.0
    grad_q = []
    grad_k = 0.0
    grad_v = 0.0
    for (first, last), part, two, rows, logs in zip(cuts, grads, two_terms, hidden, log_total):
        normed, inverse = norm_forward(rows, gains[1], shifts[2])[1:]
        moved, gain_part, shift_part = norm_backward(two, normed, inverse, gains[1])
        gain_two += gain_part
        shift_two += shift_part
        grad_hidden.append(part.astype(F32) + moved)
        grad_attn.append(grad_hidden[-1].astype(BF16))
        attn_shift += jnp.sum(grad_attn[-1].astype(F32), axis=0)
        grad_context = dot_nn(grad_attn[-1], out_t).astype(BF16).reshape(last - first, -1, HD)
        scores = (
            jnp.einsum("qhd,khd->hqk", queries[first:last], key_rows, preferred_element_type=F32)
            * scale
        )
        probs = jnp.exp(scores - logs)
        probs = jnp.where(lax.broadcasted_iota(jnp.int32, scores.shape, 2) < real, probs, 0.0)
        mixed = jnp.einsum("qhd,khd->hqk", grad_context, values, preferred_element_type=F32)
        row_delta = jnp.sum(mixed * probs, axis=-1, keepdims=True)
        grad_scores = (probs * (mixed - row_delta)).astype(BF16)
        grad_v += jnp.einsum("hqk,qhd->khd", probs.astype(BF16), grad_context, preferred_element_type=F32)
        grad_q.append(
            (jnp.einsum("hqk,khd->qhd", grad_scores, key_rows, preferred_element_type=F32) * scale).astype(BF16)
        )
        grad_k += jnp.einsum("hqk,qhd->khd", grad_scores, queries[first:last], preferred_element_type=F32)
    grad_proj = jnp.concatenate(
        [
            jnp.concatenate(grad_q).reshape(-1, width),
            (grad_k * scale).astype(BF16).reshape(-1, width),
            grad_v.astype(BF16).reshape(-1, width),
        ],
        axis=1,
    )
    context_all = jnp.concatenate(context)
    attn_all = jnp.concatenate(grad_attn)
    grad_out = dot_tn(attn_all, context_all)
    grad_qkv = dot_tn(normed_one, grad_proj)
    bias_sums = jnp.sum(grad_proj.astype(F32), axis=0)
    grad_inputs = []
    gain_one, shift_one = 0.0, 0.0
    one, grad_qkv, grad_out = line_share(
        dot_nt(grad_proj, qkv).astype(BF16), [grad_qkv.astype(BF16), grad_out.astype(BF16)], layer, 2 + 2 * layer
    )
    one_terms = [one.astype(F32)]
    for one, part, rows in zip(one_terms, inputs, grad_hidden):
        normed, inverse = norm_forward(part.astype(F32), gains[0], shifts[0])[1:]
        moved, gain_part, shift_part = norm_backward(one, normed, inverse, gains[0])
        gain_one += gain_part
        shift_one += shift_part
        grad_inputs.append((rows + moved).astype(BF16))
    gain_grads = [gain_two, attn_shift, shift_two, mix_shift]
    bias_grads = jnp.concatenate([bias_sums[:width], bias_sums[2 * width :], up_bias_grad])
    late = jnp.concatenate([gain_one, shift_one])
    return grad_inputs, extra, (grad_qkv, grad_out, grad_up, grad_down), (jnp.concatenate(gain_grads + [bias_grads]), late)


def per_device(
    images,
    cotangent,
    qkv_weight,
    qv_bias,
    out_weight,
    up_weight,
    up_bias,
    down_weight,
    gains,
    shifts,
):
    image_count, seq_len, model_width = images.shape[1:]
    rows_here = qkv_weight.shape[2]
    width = qkv_weight.shape[3]
    units = up_weight.shape[2]
    section = lax.axis_index("section")
    fsdp = lax.axis_index("fsdp")
    is_first = section == 0
    every = ("section", "fsdp")
    padded = -(-seq_len // TILE) * TILE
    cuts = [(0, padded)]

    def gathered(piece):
        whole = lax.all_gather(piece, every, axis=0, tiled=True)
        return whole.reshape(2, -1, piece.shape[1])

    gap = -3 * width % 128
    mixer = gathered(
        jnp.concatenate(
            [
                qkv_weight[0].transpose(1, 0, 2).reshape(rows_here, 3 * width),
                jnp.zeros((rows_here, gap), BF16),
                out_weight[0].T,
            ],
            axis=1,
        )
    )
    qkv = mixer[:, :, : 3 * width]
    out_t = mixer[:, :, 3 * width + gap :]
    up = gathered(up_weight[0])
    down_t = gathered(down_weight[0].T)
    scales = lax.all_gather(
        jnp.concatenate([gains[0], shifts[0]]), every, axis=0, tiled=False
    )
    scales = scales.reshape(2, -1, 6, rows_here).transpose(0, 2, 1, 3).reshape(2, 6, model_width)
    scales = scales.astype(F32)
    biases = lax.all_gather(
        jnp.concatenate([qv_bias.reshape(-1), up_bias.reshape(-1)]), "section", axis=0
    ).astype(F32)

    def padded_rows(array):
        rows = lax.dynamic_index_in_dim(array, section, 0, keepdims=False)[0]
        return jnp.pad(rows, ((0, padded - seq_len), (0, 0)))

    def layer_args(index):
        return (qkv[index], out_t[index], up[index], down_t[index])

    own = padded_rows(images)
    own_grad = padded_rows(cotangent)
    rows = [own[first:last] for first, last in cuts]
    outputs, stored = [], []
    for index in range(2):
        qv = biases[index, : 2 * width].reshape(2, width)
        rows, kept, last_term = layer_forward(
            rows, layer_args(index), qv, biases[index, 2 * width :], scales[index, :2], scales[index, 2:], cuts, seq_len, index == 1
        )
        outputs.append(rows[0])
        stored.append(kept)

    def swapped(pair):
        pair = [item[:seq_len] for item in pair]
        mine = jnp.where(is_first, pair[0], pair[1])
        other = lax.ppermute(jnp.where(is_first, pair[1], pair[0]), "section", [(0, 1), (1, 0)])
        return jnp.where(
            is_first, jnp.stack([mine, other]), jnp.stack([other, mine])
        )[None, :, None]

    grads = [own_grad[first:last] for first, last in cuts]
    input_grads = [None, None]
    weight_grads = [None, None]
    small = [None, None]
    for index in (1, 0):
        grads, total, weight_grads[index], small[index] = layer_backward(
            grads,
            stored[index],
            layer_args(index),
            scales[index, :2],
            scales[index, 2:],
            cuts,
            seq_len,
            index,
            last_term if index == 1 else None,
        )
        if index == 1:
            section_outputs = swapped([outputs[0], outputs[1](total)])
        input_grads[index] = jnp.concatenate(grads)
    input_grads = swapped(input_grads)

    grad_qkv, grad_out, grad_up, grad_down = [
        jnp.where(is_first, first, second) for first, second in zip(*weight_grads)
    ]
    packed = lax.psum(jnp.stack([small[0][0], small[1][0]]), every)
    late = lax.psum(jnp.stack([small[0][1], small[1][1]]), every)
    packed = jnp.where(is_first, packed[0], packed[1])
    late = jnp.where(is_first, late[0], late[1]).reshape(2, model_width)
    norm_part = packed[: 4 * model_width].reshape(4, model_width)
    norm_part = jnp.stack([late[0], norm_part[0], late[1], norm_part[1], norm_part[2], norm_part[3]])
    norm_part = lax.dynamic_slice_in_dim(norm_part, fsdp * rows_here, rows_here, 1)
    bias_part = packed[4 * model_width :]
    return (
        section_outputs,
        input_grads,
        grad_qkv.reshape(rows_here, 3, width).transpose(1, 0, 2)[None],
        bias_part[: 2 * width].reshape(1, 2, width),
        grad_out.T[None],
        grad_up[None],
        bias_part[2 * width :][None],
        grad_down.T[None],
        norm_part[:2][None],
        norm_part[2:][None],
    )


def solution(mesh):
    return jax.shard_map(
        per_device,
        mesh=mesh,
        in_specs=(
            P(None, "fsdp", None, None),
            P(None, "fsdp", None, None),
            P("section", None, "fsdp", "tensor"),
            P("section", None, "tensor"),
            P("section", "tensor", "fsdp"),
            P("section", "fsdp", "tensor"),
            P("section", "tensor"),
            P("section", "tensor", "fsdp"),
            P("section", None, "fsdp"),
            P("section", None, "fsdp"),
        ),
        out_specs=(
            P("section", None, "fsdp", None, None),
            P("section", None, "fsdp", None, None),
            P("section", None, "fsdp", "tensor"),
            P("section", None, "tensor"),
            P("section", "tensor", "fsdp"),
            P("section", "fsdp", "tensor"),
            P("section", "tensor"),
            P("section", "tensor", "fsdp"),
            P("section", None, "fsdp"),
            P("section", None, "fsdp"),
        ),
        check_vma=False,
    )
```

```python
import functools

import jax
import jax.numpy as jnp
from jax import lax
from jax.experimental import pallas as pl
from jax.experimental.pallas import tpu as pltpu
from jax.sharding import PartitionSpec as P
from jax.experimental.layout import Layout, with_layout_constraint

HD = 72


NORM_EPS = 1e-06
GELU_ROOT = 0.7978845608028654
GELU_CUBIC = 0.044715
F32 = jnp.float32
BF16 = jnp.bfloat16


MESH = pl.DeviceIdType.MESH
TILE = 16


def greet(me, count, others=()):
    barrier = pltpu.get_barrier_semaphore()
    for there, other in ((me > 0, me - 1), (me < count - 1, me + 1)):
        @pl.when(there)
        def _():
            pl.semaphore_signal(barrier, inc=1, device_id={"tensor": other}, device_id_type=MESH)
    for other in others:
        pl.semaphore_signal(barrier, inc=1, device_id=other, device_id_type=MESH)
    peers = (me > 0).astype(jnp.int32) + (me < count - 1).astype(jnp.int32)
    pl.semaphore_wait(barrier, peers + len(others))


class Line:
    def __init__(self, count, rows, lag, x_ref, o_ref, come, gone, sems):
        self.count, self.rows, self.lag = count, rows, lag
        self.x, self.o, self.come, self.gone = x_ref, o_ref, come, gone
        self.red, self.out = sems[:2], sems[2:]
        self.me = lax.axis_index("tensor")
        self.pieces = x_ref.shape[0] // rows
        self.pairs = (self.pieces + 1) // 2
        self.turns = self.pairs + 2 * lag * (count - 1)

    def span(self, piece):
        return pl.ds(pl.multiple_of(piece * self.rows, self.rows), self.rows)

    def send(self, piece, source, target, step, sems):
        return pltpu.make_async_remote_copy(
            src_ref=source.at[self.span(piece)],
            dst_ref=target.at[self.span(piece)],
            send_sem=sems[0].at[piece],
            recv_sem=sems[1].at[piece],
            device_id={"tensor": self.me + step},
            device_id_type=MESH,
        )

    def place(self, step):
        return self.me if step > 0 else self.count - 1 - self.me

    def reduce_step(self, index, step):
        piece = 2 * index + (step < 0)
        ok = (index >= 0) & (piece < self.pieces)
        pos = self.place(step)
        end = self.count - 1
        span = self.span(piece)

        @pl.when(ok & (pos == 0))
        def _():
            self.send(piece, self.x, self.come, step, self.red).start()

        def add():
            self.send(piece, self.come, self.come, step, self.red).wait_recv()
            return (self.x[span, :].astype(F32) + self.come[span, :].astype(F32)).astype(BF16)

        @pl.when(ok & (pos > 0) & (pos < end))
        def _():
            self.gone[span, :] = add()
            self.send(piece, self.gone, self.come, step, self.red).start()

        @pl.when(ok & (pos == end))
        def _():
            self.o[span, :] = add()
            self.send(piece, self.o, self.o, -step, self.out).start()

    def out_step(self, index, step):
        piece = 2 * index + (step < 0)
        ok = (index >= 0) & (piece < self.pieces)
        pos = self.place(step)

        @pl.when(ok & (pos < self.count - 1))
        def _():
            self.send(piece, self.o, self.o, -step, self.out).wait_recv()

        @pl.when(ok & (pos > 0) & (pos < self.count - 1))
        def _():
            self.send(piece, self.o, self.o, -step, self.out).start()

    def turn(self, s):
        for step in (1, -1):
            self.reduce_step(s - self.lag * self.place(step), step)
        back = self.lag * (self.count - 1)
        for step in (1, -1):
            self.out_step(s - back - self.lag * (self.count - 1 - self.place(step)), step)

    def finish(self):
        def end_steps(i, _):
            for step in (1, -1):
                piece = 2 * i + (step < 0)
                pos = self.place(step)

                @pl.when((piece < self.pieces) & (pos < self.count - 1))
                def _():
                    self.send(piece, self.x, self.come, step, self.red).wait_send()

                @pl.when((piece < self.pieces) & (pos > 0))
                def _():
                    self.send(piece, self.o, self.o, -step, self.out).wait_send()
            return 0

        lax.fori_loop(0, self.pairs, end_steps, 0)

    @staticmethod
    def scratch(x, rows):
        return [pltpu.VMEM(x.shape, BF16)] * 2 + [pltpu.SemaphoreType.DMA((x.shape[0] // rows,))] * 4


class Share:
    def __init__(self, ways, layer, cuts, g_ref, o_ref, bufs):
        self.ways, self.layer, self.cuts = ways, layer, cuts
        self.levels = ways.bit_length() - 1
        self.g, self.o = g_ref, o_ref
        n = self.levels
        self.recv, self.stage = bufs[:n], [None] + list(bufs[n : 2 * n - 1])
        bufs = bufs[2 * n - 1 :]
        self.last_recv, self.last_stage = bufs[:2]
        sems = bufs[2:]
        self.sems = [(sems[2 * j], sems[2 * j + 1]) for j in range(n + 1)]
        self.me = lax.axis_index("fsdp")
        self.owner = lax.axis_index("section") == layer
        self.height = o_ref.shape[0]
        self.rows = self.height // cuts

    def others(self):
        return [{"fsdp": self.flip(j)} for j in range(self.levels)] + [
            {"section": 1 - lax.axis_index("section")}
        ]

    def flip(self, level):
        bit = self.me // (1 << level) % 2
        return self.me + (1 - 2 * bit) * (1 << level)

    def blocks(self, level):
        low = self.flip(level) % (1 << (level + 1))
        return [low + (high << (level + 1)) for high in range(self.ways >> (level + 1))]

    def span(self, piece):
        return pl.ds(pl.multiple_of(piece * self.rows, self.rows), self.rows)

    def own(self, block, piece):
        if len(self.g.shape) == 3:
            return self.g.at[block, self.span(piece)]
        return self.g.at[pl.ds(pl.multiple_of(block * self.height + piece * self.rows, self.rows), self.rows)]

    def copy(self, level, block, piece):
        place = block // (1 << (level + 1))
        return pltpu.make_async_remote_copy(
            src_ref=self.own(block, piece) if level == 0 else self.stage[level].at[place, self.span(piece)],
            dst_ref=self.recv[level].at[place, self.span(piece)],
            send_sem=self.sems[level][0].at[place * self.cuts + piece],
            recv_sem=self.sems[level][1].at[place * self.cuts + piece],
            device_id={"fsdp": self.flip(level)},
            device_id_type=MESH,
        )

    def last_copy(self, piece):
        return pltpu.make_async_remote_copy(
            src_ref=self.last_stage.at[self.span(piece)],
            dst_ref=self.last_recv.at[self.span(piece)],
            send_sem=self.sems[-1][0].at[piece],
            recv_sem=self.sems[-1][1].at[piece],
            device_id={"section": 1 - lax.axis_index("section")},
            device_id_type=MESH,
        )

    def start(self):
        for piece in range(self.cuts):
            for block in self.blocks(0):
                self.copy(0, block, piece).start()

    def total(self, level, block, piece):
        value = self.own(block, piece)[...].astype(F32)
        for j in range(level):
            self.copy(j, block, piece).wait_recv()
            value += self.recv[j][block // (1 << (j + 1)), self.span(piece), :].astype(F32)
        return value

    def step(self, level, piece):
        if level < self.levels:
            for block in self.blocks(level):
                self.stage[level][block // (1 << (level + 1)), self.span(piece), :] = self.total(
                    level, block, piece
                ).astype(BF16)
                self.copy(level, block, piece).start()
        elif level == self.levels:
            value = self.total(level, self.me, piece)
            self.o[self.span(piece), :] = value

            @pl.when(jnp.logical_not(self.owner))
            def _():
                self.last_stage[self.span(piece), :] = value.astype(BF16)
                self.last_copy(piece).start()
        else:

            @pl.when(self.owner)
            def _():
                self.last_copy(piece).wait_recv()
                self.o[self.span(piece), :] += self.last_recv[self.span(piece), :].astype(F32)

    def finish(self):
        for piece in range(self.cuts):
            for level in range(self.levels):
                for block in self.blocks(level):
                    self.copy(level, block, piece).wait_send()

            @pl.when(jnp.logical_not(self.owner))
            def _():
                self.last_copy(piece).wait_send()

    @staticmethod
    def scratch(shape, ways, cuts):
        levels = ways.bit_length() - 1
        rows, width = shape
        counts = [ways >> (j + 1) for j in range(levels)]
        sems = []
        for count in counts + [1]:
            sems += [pltpu.SemaphoreType.DMA((count * cuts,))] * 2
        return (
            [pltpu.VMEM((count, rows, width), BF16) for count in counts + counts[1:]]
            + [pltpu.VMEM((rows, width), BF16)] * 2
            + sems
        )


def line_sum_kernel(count, rows, lag, x_ref, o_ref, come, gone, *sems):
    line = Line(count, rows, lag, x_ref, o_ref, come, gone, sems)
    greet(line.me, count)
    lax.fori_loop(0, line.turns, lambda s, _: (line.turn(s), 0)[1], 0)
    line.finish()


def line_sum(x, cid, rows=16, lag=4):
    count = lax.axis_size("tensor")
    return pl.pallas_call(
        functools.partial(line_sum_kernel, count, rows, lag),
        out_shape=jax.ShapeDtypeStruct(x.shape, BF16),
        in_specs=[pl.BlockSpec(memory_space=pltpu.VMEM)],
        out_specs=pl.BlockSpec(memory_space=pltpu.VMEM),
        scratch_shapes=Line.scratch(x, rows),
        compiler_params=pltpu.CompilerParams(collective_id=cid, has_side_effects=True),
        name="line_sum",
        cost_estimate=pl.CostEstimate(flops=0, bytes_accessed=120_000_000, transcendentals=0),
    )(x)


class Swap:
    def __init__(self, line, layer, refs, outs, bufs):
        self.line, self.layer = line, layer
        self.u, self.grad, self.gain, self.ready = refs
        self.mine, self.got, self.late = outs
        self.sems = bufs[:2]
        self.small = Small(self.late, self.late, bufs[2:])
        self.section = lax.axis_index("section")
        self.first = 2 * line.lag * (line.count - 1)
        self.steps = line.pieces // 2
        self.rows = 2 * line.rows

    def span(self, index):
        return pl.ds(pl.multiple_of(index * self.rows, self.rows), self.rows)

    def copy(self, source, index):
        return pltpu.make_async_remote_copy(
            src_ref=source.at[self.span(index)],
            dst_ref=self.got.at[self.span(index)],
            send_sem=self.sems[0].at[index],
            recv_sem=self.sems[1].at[index],
            device_id={"section": 1 - self.section},
            device_id_type=MESH,
        )

    def start(self):
        self.late[...] = jnp.zeros_like(self.late)

    def step(self, index):
        span = self.span(index)
        one = self.line.o[span, :].astype(F32)
        _, normed, inverse = norm_forward(self.u[span, :].astype(F32), 1.0, 0.0)
        moved, gain_part, shift_part = norm_backward(one, normed, inverse, self.gain[...])
        self.mine[span, :] = (self.grad[span, :] + moved).astype(BF16)
        self.late[0:1, :] += gain_part.reshape(1, -1)
        self.late[1:2, :] += shift_part.reshape(1, -1)

        @pl.when(self.section == self.layer)
        def _():
            self.copy(self.ready, index).start()

        @pl.when(self.section != self.layer)
        def _():
            self.copy(self.mine, index).start()

    def finish(self):
        for level in range(self.small.levels + 2):
            self.small.step(level)

        def end_steps(index, _):
            @pl.when(self.section == self.layer)
            def _():
                self.copy(self.ready, index).wait_send()

            @pl.when(self.section != self.layer)
            def _():
                self.copy(self.mine, index).wait_send()

            self.copy(self.got, index).wait_recv()
            return 0

        lax.fori_loop(0, self.steps, end_steps, 0)
        self.small.finish()

    @staticmethod
    def scratch(x, ways, rows):
        return Pass.scratch(x, rows) + Small.scratch((8, x.shape[1]), ways)


class Pass:
    def __init__(self, line, pair, got, sems):
        self.pair, self.got, self.sems = pair, got, sems
        self.section = lax.axis_index("section")
        self.rows = 2 * line.rows
        self.steps = got.shape[0] // self.rows

    def copy(self, source, index):
        span = pl.ds(pl.multiple_of(index * self.rows, self.rows), self.rows)
        return pltpu.make_async_remote_copy(
            src_ref=source.at[span],
            dst_ref=self.got.at[span],
            send_sem=self.sems[0].at[index],
            recv_sem=self.sems[1].at[index],
            device_id={"section": 1 - self.section},
            device_id_type=MESH,
        )

    def step(self, index):
        for place in range(2):

            @pl.when(self.section == 1 - place)
            def _():
                self.copy(self.pair[place], index).start()

    def finish(self):
        def end_steps(index, _):
            for place in range(2):

                @pl.when(self.section == 1 - place)
                def _():
                    self.copy(self.pair[place], index).wait_send()

            self.copy(self.got, index).wait_recv()
            return 0

        lax.fori_loop(0, self.steps, end_steps, 0)

    @staticmethod
    def scratch(x, rows):
        return [pltpu.SemaphoreType.DMA((x.shape[0] // (2 * rows),))] * 2


class Small:
    def __init__(self, value, total, bufs):
        self.value, self.total = value, total
        self.levels = lax.axis_size("fsdp").bit_length() - 1
        n = self.levels + 1
        self.away, self.near, self.sems = bufs[:n], bufs[n : 2 * n], bufs[2 * n :]

    def copy(self, level):
        me = lax.axis_index("fsdp")
        if level < self.levels:
            there = {"fsdp": me + (1 - 2 * (me // (1 << level) % 2)) * (1 << level)}
        else:
            there = {"section": 1 - lax.axis_index("section")}
        return pltpu.make_async_remote_copy(
            src_ref=self.away[level],
            dst_ref=self.near[level],
            send_sem=self.sems[0].at[level],
            recv_sem=self.sems[1].at[level],
            device_id=there,
            device_id_type=MESH,
        )

    def step(self, level):
        if level == 0:
            now = self.value[...]
        else:
            self.copy(level - 1).wait_recv()
            now = self.away[level - 1][...] + self.near[level - 1][...]
        if level > self.levels:
            self.total[...] = now
        else:
            self.away[level][...] = now
            self.copy(level).start()

    def finish(self):
        for level in range(self.levels + 1):
            self.copy(level).wait_send()

    @staticmethod
    def scratch(shape, ways):
        n = ways.bit_length()
        return [pltpu.VMEM(shape, F32)] * (2 * n) + [pltpu.SemaphoreType.DMA((n,))] * 2


def line_share_kernel(count, rows, lag, ways, layer, cuts, k, trade, small, passing, *refs):
    refs = list(refs)

    def take(number):
        taken, refs[:] = refs[:number], refs[number:]
        return taken

    x_ref, g_refs = take(1)[0], take(k)
    swap_refs, small_ref, pair = take(4 * trade), take(small), take(2 * passing)
    go_refs = take(k)
    swap_outs, small_out, got = take(3 * trade), take(small), take(passing)
    o_ref = take(1)[0]
    line = Line(count, rows, lag, x_ref, o_ref, *take(2), take(4))
    swap, extra = None, []
    each = 2 * ways.bit_length() + 2
    if trade:
        swap = Swap(line, layer, swap_refs, swap_outs, take(2 + each))
        swap.start()
    if small:
        sums = Small(small_ref[0], small_out[0], take(each))
        extra.append(sums)
    if passing:
        pass_on = Pass(line, pair, got[0], take(2))
        extra.append(pass_on)
    scratch = refs
    each = len(scratch) // k
    shares = [
        Share(ways, layer, cuts, g_refs[i], go_refs[i], scratch[i * each : (i + 1) * each]) for i in range(k)
    ]
    levels = shares[0].levels
    greet(line.me, count, shares[0].others())
    for share in shares:
        share.start()
    steps = []
    for level in range(1, levels + 2):
        first, stride = (4, 1) if level == 1 else (3 + 6 * (level - 1), 5)
        steps += [(first + i * cuts * stride, stride, level, share) for i, share in enumerate(shares)]
    if trade:
        steps.append((swap.first, 1, 0, swap))
    turns = max(line.turns, max(first + stride * (cuts - 1) + 1 for first, stride, _, item in steps if item is not swap))

    def turn(s, _):
        line.turn(s)
        if small:
            for level in range(levels + 2):

                @pl.when(s == 6 * level + 2)
                def _():
                    sums.step(level)

        if passing:

            @pl.when((s % 2 == 0) & (s // 2 < pass_on.steps))
            def _():
                pass_on.step(s // 2)

        for first, stride, level, share in steps:
            past = s - first
            piece = past // stride

            if share is swap:

                @pl.when((past >= 0) & (past < swap.steps))
                def _():
                    swap.step(past)

                continue

            @pl.when((past >= 0) & (past % stride == 0) & (piece < cuts))
            def _():
                share.step(level, piece)
        return 0

    if small:
        turns = max(turns, 6 * (levels + 2) + 1)
    if passing:
        turns = max(turns, 2 * pass_on.steps)
    lax.fori_loop(0, turns, turn, 0)
    if trade:
        swap.finish()
    for item in extra:
        item.finish()
    line.finish()
    for share in shares:
        share.finish()


def line_share(x, grads, layer, cid, trade=(), small=None, pair=(), rows=16, lag=4):
    count, ways = lax.axis_size("tensor"), lax.axis_size("fsdp")
    height = grads[0].shape[0] // ways
    shapes = [(height, g.shape[1]) for g in grads]
    cuts = 3 if height % (3 * TILE) == 0 else 1
    if height % TILE:
        grads = [g.reshape(ways, height, g.shape[1]) for g in grads]
    total = jax.ShapeDtypeStruct(x.shape, BF16)
    scratch = Line.scratch(x, rows)
    outs = [jax.ShapeDtypeStruct(shape, F32) for shape in shapes]
    args = [x, *grads, *trade]
    if trade:
        outs += [total, total, jax.ShapeDtypeStruct((8, x.shape[1]), F32)]
        scratch += Swap.scratch(x, ways, rows)
    if small is not None:
        args.append(small)
        outs.append(jax.ShapeDtypeStruct(small.shape, F32))
        scratch += Small.scratch(small.shape, ways)
    if pair:
        args += pair
        outs.append(total)
        scratch += Pass.scratch(x, rows)
    if trade:
        scratch = [pltpu.VMEM(x.shape, BF16)] + scratch
    else:
        outs.append(total)
    for shape in shapes:
        scratch += Share.scratch(shape, ways, cuts)
    vmem = pl.BlockSpec(memory_space=pltpu.VMEM)
    return pl.pallas_call(
        functools.partial(
            line_share_kernel,
            count,
            rows,
            lag,
            ways,
            layer,
            cuts,
            len(grads),
            bool(trade),
            small is not None,
            bool(pair),
        ),
        out_shape=outs,
        in_specs=[vmem] * len(args),
        out_specs=[vmem] * len(outs),
        scratch_shapes=scratch,
        compiler_params=pltpu.CompilerParams(
            collective_id=cid, has_side_effects=True, vmem_limit_bytes=60 * 1024 * 1024
        ),
        name="line_share",
        cost_estimate=pl.CostEstimate(flops=0, bytes_accessed=120_000_000, transcendentals=0),
    )(*args)


def tensor_sum(value):
    return line_sum(value.astype(BF16), 0).astype(F32)


def gelu_value(value):
    return 0.5 * value * (1.0 + jnp.tanh(GELU_ROOT * (value + GELU_CUBIC * value * value * value)))


def gelu_slope(value):
    inner = jnp.tanh(GELU_ROOT * (value + GELU_CUBIC * value * value * value))
    return 0.5 * (1.0 + inner) + 0.5 * value * (1.0 - inner * inner) * GELU_ROOT * (
        1.0 + 3.0 * GELU_CUBIC * value * value
    )


def norm_forward(token_rows, gain, shift):
    mean_row = jnp.mean(token_rows, axis=-1, keepdims=True)
    centred = token_rows - mean_row
    inverse = lax.rsqrt(jnp.mean(centred * centred, axis=-1, keepdims=True) + NORM_EPS)
    normed = centred * inverse
    return (normed * gain + shift, normed, inverse)


def norm_backward(grad_normed, normed, inverse, gain):
    scaled = grad_normed * gain
    inner = (
        scaled
        - jnp.mean(scaled, axis=-1, keepdims=True)
        - normed * jnp.mean(scaled * normed, axis=-1, keepdims=True)
    )
    return (inverse * inner, jnp.sum(grad_normed * normed, axis=0), jnp.sum(grad_normed, axis=0))


def dot_nn(left, right):
    return jnp.dot(left, right, preferred_element_type=F32)


def dot_nt(left, right):
    return lax.dot_general(left, right, (((1,), (1,)), ((), ())), preferred_element_type=F32)


def dot_tn(left, right):
    return with_layout_constraint(lax.dot_general(left, right, (((0,), (0,)), ((), ())), preferred_element_type=F32), Layout((0,1)))


def layer_forward(inputs, weights, qv_bias, up_bias, gains, shifts, cuts, real, is_last):
    qkv, out_t, up, down_t = weights
    width = qkv.shape[1] // 3
    heads = width // HD
    scale = HD ** (-0.5)
    seq_len = cuts[-1][1]
    normed_one = []
    parts = []
    for part in inputs:
        normed = norm_forward(part.astype(F32), gains[0], shifts[0])[0].astype(BF16)
        normed_one.append(normed)
        parts.append(dot_nn(normed, qkv))
    normed_one = jnp.concatenate(normed_one)
    projected = jnp.concatenate(parts)
    queries = (projected[:, :width] + qv_bias[0]).astype(BF16).reshape(seq_len, heads, HD)
    key_rows = projected[:, width : 2 * width].astype(BF16).reshape(seq_len, heads, HD)
    values = (projected[:, 2 * width :] + qv_bias[1]).astype(BF16).reshape(seq_len, heads, HD)
    context, hidden, normed_two, pre_act, active, outputs, log_total = [], [], [], [], [], [], []
    for (first, last), part in zip(cuts, inputs):
        scores = (
            jnp.einsum("qhd,khd->hqk", queries[first:last], key_rows, preferred_element_type=F32)
            * scale
        )
        scores = jnp.where(lax.broadcasted_iota(jnp.int32, scores.shape, 2) < real, scores, -1e30)
        row_max = jnp.max(scores, axis=-1, keepdims=True)
        exp_scores = jnp.exp(scores - row_max)
        row_total = jnp.sum(exp_scores, axis=-1, keepdims=True)
        probs = (exp_scores / row_total).astype(BF16)
        log_total.append(row_max + jnp.log(row_total))
        mixed = jnp.einsum("hqk,khd->qhd", probs, values, preferred_element_type=F32)
        context.append(mixed.astype(BF16).reshape(last - first, width))
        attn_term = tensor_sum(dot_nt(context[-1], out_t))
        hidden.append(part.astype(F32) + attn_term + shifts[1])
    for rows in hidden:
        normed = norm_forward(rows, gains[1], shifts[2])[0].astype(BF16)
        normed_two.append(normed)
        pre_act.append(dot_nn(normed, up) + up_bias)
        active.append(gelu_value(pre_act[-1]).astype(BF16))
        mlp_term = dot_nt(active[-1], down_t).astype(BF16)
        if is_last:
            outputs.append(None)
            stored_term = mlp_term
            continue
        outputs.append((rows + line_sum(mlp_term, 0).astype(F32) + shifts[3]).astype(BF16))
        stored_term = None
    stored = (
        inputs,
        normed_one,
        queries,
        key_rows,
        values,
        log_total,
        context,
        hidden,
        normed_two,
        pre_act,
        active,
    )
    return outputs, stored, stored_term


def layer_backward(grads, stored, weights, gains, shifts, cuts, real, layer, extra, ready, small):
    qkv, out_t, up, down_t = weights
    (
        inputs,
        normed_one,
        queries,
        key_rows,
        values,
        log_total,
        context,
        hidden,
        normed_two,
        pre_act,
        active,
    ) = stored
    width = qkv.shape[1] // 3
    scale = HD ** (-0.5)
    grad_mix = [part.astype(BF16) for part in grads]
    grad_pre = []
    two_terms = []
    for part, pre in zip(grad_mix, pre_act):
        grad_active = dot_nn(part, down_t)
        grad_pre.append((grad_active * gelu_slope(pre)).astype(BF16))
        two_terms.append(dot_nt(grad_pre[-1], up).astype(BF16))
    mix_all = jnp.concatenate(grad_mix)
    pre_all = jnp.concatenate(grad_pre)
    grad_down = dot_tn(mix_all, jnp.concatenate(active))
    grad_up = dot_tn(jnp.concatenate(normed_two), pre_all)
    count = two_terms[0].shape[0]
    extra_rows, last_shift = hidden[0], shifts[3]
    two = two_terms[0] if extra is None else jnp.concatenate([two_terms[0], extra])
    grad_down, grad_up, two = line_share(
        two, [grad_down.astype(BF16), grad_up.astype(BF16)], layer, 1 + 2 * layer
    )
    two_terms = [two[:count].astype(F32)]
    extra = two[count:]
    up_bias_grad = jnp.sum(pre_all.astype(F32), axis=0)
    mix_shift = jnp.sum(mix_all.astype(F32), axis=0)
    grad_hidden, grad_attn, gain_two, shift_two, attn_shift = [], [], 0.0, 0.0, 0.0
    grad_q = []
    grad_k = 0.0
    grad_v = 0.0
    for (first, last), part, two, rows, logs in zip(cuts, grads, two_terms, hidden, log_total):
        normed, inverse = norm_forward(rows, gains[1], shifts[2])[1:]
        moved, gain_part, shift_part = norm_backward(two, normed, inverse, gains[1])
        gain_two += gain_part
        shift_two += shift_part
        grad_hidden.append(part.astype(F32) + moved)
        grad_attn.append(grad_hidden[-1].astype(BF16))
        attn_shift += jnp.sum(grad_attn[-1].astype(F32), axis=0)
        grad_context = dot_nn(grad_attn[-1], out_t).astype(BF16).reshape(last - first, -1, HD)
        scores = (
            jnp.einsum("qhd,khd->hqk", queries[first:last], key_rows, preferred_element_type=F32)
            * scale
        )
        probs = jnp.exp(scores - logs)
        probs = jnp.where(lax.broadcasted_iota(jnp.int32, scores.shape, 2) < real, probs, 0.0)
        mixed = jnp.einsum("qhd,khd->hqk", grad_context, values, preferred_element_type=F32)
        row_delta = jnp.sum(mixed * probs, axis=-1, keepdims=True)
        grad_scores = (probs * (mixed - row_delta)).astype(BF16)
        grad_v += jnp.einsum("hqk,qhd->khd", probs.astype(BF16), grad_context, preferred_element_type=F32)
        grad_q.append(
            (jnp.einsum("hqk,khd->qhd", grad_scores, key_rows, preferred_element_type=F32) * scale).astype(BF16)
        )
        grad_k += jnp.einsum("hqk,qhd->khd", grad_scores, queries[first:last], preferred_element_type=F32)
    grad_proj = jnp.concatenate(
        [
            jnp.concatenate(grad_q).reshape(-1, width),
            (grad_k * scale).astype(BF16).reshape(-1, width),
            grad_v.astype(BF16).reshape(-1, width),
        ],
        axis=1,
    )
    context_all = jnp.concatenate(context)
    attn_all = jnp.concatenate(grad_attn)
    grad_out = dot_tn(attn_all, context_all)
    grad_qkv = dot_tn(normed_one, grad_proj)
    bias_sums = jnp.sum(grad_proj.astype(F32), axis=0)
    send = [dot_nt(grad_proj, qkv).astype(BF16), [grad_qkv.astype(BF16), grad_out.astype(BF16)], layer, 2 + 2 * layer]
    sums = [gain_two, attn_shift, shift_two, mix_shift]
    sums += [bias_sums[:width], bias_sums[2 * width :], up_bias_grad]
    late = other = None
    if ready is not None:
        sums = jnp.concatenate(sums + small)
        sums = jnp.pad(sums, (0, -sums.shape[0] % (8 * part.shape[1]))).reshape(-1, part.shape[1])
        trade = (inputs[0], grad_hidden[0], gains[:1], ready)
        grad_qkv, grad_out, mine, other, late, sums = line_share(*send, trade, sums)
    else:
        first = inputs[0]
        last = (extra_rows + extra.astype(F32) + last_shift).astype(BF16)
        grad_qkv, grad_out, other, one = line_share(*send, pair=(first, last))
        other = (first, last, other)
        normed, inverse = norm_forward(inputs[0].astype(F32), gains[0], shifts[0])[1:]
        moved, gain_one, shift_one = norm_backward(one.astype(F32), normed, inverse, gains[0])
        mine = (grad_hidden[0] + moved).astype(BF16)
        sums += [gain_one, shift_one]
    return mine, other, (grad_qkv, grad_out, grad_up, grad_down), sums, late


def per_device(
    images,
    cotangent,
    qkv_weight,
    qv_bias,
    out_weight,
    up_weight,
    up_bias,
    down_weight,
    gains,
    shifts,
):
    image_count, seq_len, model_width = images.shape[1:]
    rows_here = qkv_weight.shape[2]
    width = qkv_weight.shape[3]
    units = up_weight.shape[2]
    section = lax.axis_index("section")
    fsdp = lax.axis_index("fsdp")
    is_first = section == 0
    every = ("section", "fsdp")
    padded = -(-seq_len // TILE) * TILE
    cuts = [(0, padded)]

    def gathered(piece):
        whole = lax.all_gather(piece, every, axis=0, tiled=True)
        return whole.reshape(2, -1, piece.shape[1])

    gap = -3 * width % 128
    mixer = gathered(
        jnp.concatenate(
            [
                qkv_weight[0].transpose(1, 0, 2).reshape(rows_here, 3 * width),
                jnp.zeros((rows_here, gap), BF16),
                out_weight[0].T,
            ],
            axis=1,
        )
    )
    qkv = mixer[:, :, : 3 * width]
    out_t = mixer[:, :, 3 * width + gap :]
    up = gathered(up_weight[0])
    down_t = gathered(down_weight[0].T)
    scales = lax.all_gather(
        jnp.concatenate([gains[0], shifts[0]]), every, axis=0, tiled=False
    )
    scales = scales.reshape(2, -1, 6, rows_here).transpose(0, 2, 1, 3).reshape(2, 6, model_width)
    scales = scales.astype(F32)
    biases = lax.all_gather(
        jnp.concatenate([qv_bias.reshape(-1), up_bias.reshape(-1)]), "section", axis=0
    ).astype(F32)

    def padded_rows(array):
        rows = lax.dynamic_index_in_dim(array, section, 0, keepdims=False)[0]
        return jnp.pad(rows, ((0, padded - seq_len), (0, 0)))

    def layer_args(index):
        return (qkv[index], out_t[index], up[index], down_t[index])

    own = padded_rows(images)
    own_grad = padded_rows(cotangent)
    rows = [own[first:last] for first, last in cuts]
    outputs, stored = [], []
    for index in range(2):
        qv = biases[index, : 2 * width].reshape(2, width)
        rows, kept, last_term = layer_forward(
            rows, layer_args(index), qv, biases[index, 2 * width :], scales[index, :2], scales[index, 2:], cuts, seq_len, index == 1
        )
        outputs.append(rows[0])
        stored.append(kept)

    def placed(mine, other):
        mine, other = mine[:seq_len], other[:seq_len]
        return jnp.where(is_first, jnp.stack([mine, other]), jnp.stack([other, mine]))[None, :, None]

    grads = [own_grad[first:last] for first, last in cuts]
    input_grads = [None, None]
    weight_grads = [None, None]
    small = ready = None
    for index in (1, 0):
        mine, other, weight_grads[index], small, late = layer_backward(
            grads,
            stored[index],
            layer_args(index),
            scales[index, :2],
            scales[index, 2:],
            cuts,
            seq_len,
            index,
            last_term if index == 1 else None,
            ready,
            small,
        )
        if index == 1:
            ready, grads = mine, [mine]
            first, last, other = other
            section_outputs = placed(jnp.where(is_first, first, last), other)
        else:
            input_grads = placed(jnp.where(is_first, mine, ready), other)
    grad_qkv, grad_out, grad_up, grad_down = [
        jnp.where(is_first, first, second) for first, second in zip(*weight_grads)
    ]
    each = 4 * model_width + 2 * width + units
    small = small.reshape(-1)
    packed = jnp.where(is_first, small[:each], small[each : 2 * each])
    late = jnp.where(is_first, late[:2], small[2 * each : 2 * each + 2 * model_width].reshape(2, model_width))
    norm_part = packed[: 4 * model_width].reshape(4, model_width)
    norm_part = jnp.stack([late[0], norm_part[0], late[1], norm_part[1], norm_part[2], norm_part[3]])
    norm_part = lax.dynamic_slice_in_dim(norm_part, fsdp * rows_here, rows_here, 1)
    bias_part = packed[4 * model_width :]
    return (
        section_outputs,
        input_grads,
        grad_qkv.reshape(rows_here, 3, width).transpose(1, 0, 2)[None],
        bias_part[: 2 * width].reshape(1, 2, width),
        grad_out.T[None],
        grad_up[None],
        bias_part[2 * width :][None],
        grad_down.T[None],
        norm_part[:2][None],
        norm_part[2:][None],
    )


def solution(mesh):
    return jax.shard_map(
        per_device,
        mesh=mesh,
        in_specs=(
            P(None, "fsdp", None, None),
            P(None, "fsdp", None, None),
            P("section", None, "fsdp", "tensor"),
            P("section", None, "tensor"),
            P("section", "tensor", "fsdp"),
            P("section", "fsdp", "tensor"),
            P("section", "tensor"),
            P("section", "tensor", "fsdp"),
            P("section", None, "fsdp"),
            P("section", None, "fsdp"),
        ),
        out_specs=(
            P("section", None, "fsdp", None, None),
            P("section", None, "fsdp", None, None),
            P("section", None, "fsdp", "tensor"),
            P("section", None, "tensor"),
            P("section", "tensor", "fsdp"),
            P("section", "fsdp", "tensor"),
            P("section", "tensor"),
            P("section", "tensor", "fsdp"),
            P("section", None, "fsdp"),
            P("section", None, "fsdp"),
        ),
        check_vma=False,
    )
```

```python
import functools

import jax
import jax.numpy as jnp
from jax import lax
from jax.experimental import pallas as pl
from jax.experimental.pallas import tpu as pltpu
from jax.sharding import PartitionSpec as P
from jax.experimental.layout import Layout, with_layout_constraint

HD = 72


NORM_EPS = 1e-06
GELU_ROOT = 0.7978845608028654
GELU_CUBIC = 0.044715
F32 = jnp.float32
BF16 = jnp.bfloat16


MESH = pl.DeviceIdType.MESH
TILE = 16


def greet(me, count, others=()):
    barrier = pltpu.get_barrier_semaphore()
    for there, other in ((me > 0, me - 1), (me < count - 1, me + 1)):
        @pl.when(there)
        def _():
            pl.semaphore_signal(barrier, inc=1, device_id={"tensor": other}, device_id_type=MESH)
    for other in others:
        pl.semaphore_signal(barrier, inc=1, device_id=other, device_id_type=MESH)
    peers = (me > 0).astype(jnp.int32) + (me < count - 1).astype(jnp.int32)
    pl.semaphore_wait(barrier, peers + len(others))


class Line:
    def __init__(self, count, rows, lag, x_ref, o_ref, come, gone, sems):
        self.count, self.rows, self.lag = count, rows, lag
        self.x, self.o, self.come, self.gone = x_ref, o_ref, come, gone
        self.red, self.out = sems[:2], sems[2:]
        self.me = lax.axis_index("tensor")
        self.pieces = x_ref.shape[0] // rows
        self.pairs = (self.pieces + 1) // 2
        self.turns = self.pairs + 2 * lag * (count - 1)

    def span(self, piece):
        return pl.ds(pl.multiple_of(piece * self.rows, self.rows), self.rows)

    def send(self, piece, source, target, step, sems):
        return pltpu.make_async_remote_copy(
            src_ref=source.at[self.span(piece)],
            dst_ref=target.at[self.span(piece)],
            send_sem=sems[0].at[piece],
            recv_sem=sems[1].at[piece],
            device_id={"tensor": self.me + step},
            device_id_type=MESH,
        )

    def place(self, step):
        return self.me if step > 0 else self.count - 1 - self.me

    def reduce_step(self, index, step):
        piece = 2 * index + (step < 0)
        ok = (index >= 0) & (piece < self.pieces)
        pos = self.place(step)
        end = self.count - 1
        span = self.span(piece)

        @pl.when(ok & (pos == 0))
        def _():
            self.send(piece, self.x, self.come, step, self.red).start()

        def add():
            self.send(piece, self.come, self.come, step, self.red).wait_recv()
            return (self.x[span, :].astype(F32) + self.come[span, :].astype(F32)).astype(BF16)

        @pl.when(ok & (pos > 0) & (pos < end))
        def _():
            self.gone[span, :] = add()
            self.send(piece, self.gone, self.come, step, self.red).start()

        @pl.when(ok & (pos == end))
        def _():
            self.o[span, :] = add()
            self.send(piece, self.o, self.o, -step, self.out).start()

    def out_step(self, index, step):
        piece = 2 * index + (step < 0)
        ok = (index >= 0) & (piece < self.pieces)
        pos = self.place(step)

        @pl.when(ok & (pos < self.count - 1))
        def _():
            self.send(piece, self.o, self.o, -step, self.out).wait_recv()

        @pl.when(ok & (pos > 0) & (pos < self.count - 1))
        def _():
            self.send(piece, self.o, self.o, -step, self.out).start()

    def turn(self, s):
        for step in (1, -1):
            self.reduce_step(s - self.lag * self.place(step), step)
        back = self.lag * (self.count - 1)
        for step in (1, -1):
            self.out_step(s - back - self.lag * (self.count - 1 - self.place(step)), step)

    def finish(self):
        def end_steps(i, _):
            for step in (1, -1):
                piece = 2 * i + (step < 0)
                pos = self.place(step)

                @pl.when((piece < self.pieces) & (pos < self.count - 1))
                def _():
                    self.send(piece, self.x, self.come, step, self.red).wait_send()

                @pl.when((piece < self.pieces) & (pos > 0))
                def _():
                    self.send(piece, self.o, self.o, -step, self.out).wait_send()
            return 0

        lax.fori_loop(0, self.pairs, end_steps, 0)

    @staticmethod
    def scratch(x, rows):
        return [pltpu.VMEM(x.shape, BF16)] * 2 + [pltpu.SemaphoreType.DMA((x.shape[0] // rows,))] * 4


class Share:
    def __init__(self, ways, layer, cuts, g_ref, o_ref, bufs):
        self.ways, self.layer, self.cuts = ways, layer, cuts
        self.levels = ways.bit_length() - 1
        self.home, self.o = g_ref, o_ref
        self.g, self.load_sem = bufs[:2]
        bufs = bufs[2:]
        n = self.levels
        self.recv, self.stage = bufs[:n], [None] + list(bufs[n : 2 * n - 1])
        bufs = bufs[2 * n - 1 :]
        self.last_recv, self.last_stage = bufs[:2]
        sems = bufs[2:]
        self.sems = [(sems[2 * j], sems[2 * j + 1]) for j in range(n + 1)]
        self.me = lax.axis_index("fsdp")
        self.owner = lax.axis_index("section") == layer
        self.height = o_ref.shape[0]
        self.rows = self.height // cuts

    def others(self):
        return [{"fsdp": self.flip(j)} for j in range(self.levels)] + [
            {"section": 1 - lax.axis_index("section")}
        ]

    def flip(self, level):
        bit = self.me // (1 << level) % 2
        return self.me + (1 - 2 * bit) * (1 << level)

    def blocks(self, level):
        low = self.flip(level) % (1 << (level + 1))
        return [low + (high << (level + 1)) for high in range(self.ways >> (level + 1))]

    def span(self, piece):
        return pl.ds(pl.multiple_of(piece * self.rows, self.rows), self.rows)

    def load(self):
        return pltpu.make_async_copy(self.home, self.g, self.load_sem)

    def own(self, array, block, piece):
        if len(array.shape) == 3:
            return array.at[block, self.span(piece)]
        return array.at[pl.ds(pl.multiple_of(block * self.height + piece * self.rows, self.rows), self.rows)]

    def copy(self, level, block, piece):
        place = block // (1 << (level + 1))
        return pltpu.make_async_remote_copy(
            src_ref=self.own(self.home, block, piece) if level == 0 else self.stage[level].at[place, self.span(piece)],
            dst_ref=self.recv[level].at[place, self.span(piece)],
            send_sem=self.sems[level][0].at[place * self.cuts + piece],
            recv_sem=self.sems[level][1].at[place * self.cuts + piece],
            device_id={"fsdp": self.flip(level)},
            device_id_type=MESH,
        )

    def last_copy(self, piece):
        return pltpu.make_async_remote_copy(
            src_ref=self.last_stage.at[self.span(piece)],
            dst_ref=self.last_recv.at[self.span(piece)],
            send_sem=self.sems[-1][0].at[piece],
            recv_sem=self.sems[-1][1].at[piece],
            device_id={"section": 1 - lax.axis_index("section")},
            device_id_type=MESH,
        )

    def start(self):
        for piece in range(self.cuts):
            for block in self.blocks(0):
                self.copy(0, block, piece).start()

    def total(self, level, block, piece):
        value = self.own(self.g, block, piece)[...].astype(F32)
        for j in range(level):
            self.copy(j, block, piece).wait_recv()
            value += self.recv[j][block // (1 << (j + 1)), self.span(piece), :].astype(F32)
        return value

    def step(self, level, piece):
        if level < self.levels:
            for block in self.blocks(level):
                self.stage[level][block // (1 << (level + 1)), self.span(piece), :] = self.total(
                    level, block, piece
                ).astype(BF16)
                self.copy(level, block, piece).start()
        elif level == self.levels:
            value = self.total(level, self.me, piece)
            self.o[self.span(piece), :] = value

            @pl.when(jnp.logical_not(self.owner))
            def _():
                self.last_stage[self.span(piece), :] = value.astype(BF16)
                self.last_copy(piece).start()
        else:

            @pl.when(self.owner)
            def _():
                self.last_copy(piece).wait_recv()
                self.o[self.span(piece), :] += self.last_recv[self.span(piece), :].astype(F32)

    def finish(self):
        for piece in range(self.cuts):
            for level in range(self.levels):
                for block in self.blocks(level):
                    self.copy(level, block, piece).wait_send()

            @pl.when(jnp.logical_not(self.owner))
            def _():
                self.last_copy(piece).wait_send()

    @staticmethod
    def scratch(g, shape, ways, cuts):
        levels = ways.bit_length() - 1
        rows, width = shape
        counts = [ways >> (j + 1) for j in range(levels)]
        sems = []
        for count in counts + [1]:
            sems += [pltpu.SemaphoreType.DMA((count * cuts,))] * 2
        return (
            [pltpu.VMEM(g.shape, BF16), pltpu.SemaphoreType.DMA]
            + [pltpu.VMEM((count, rows, width), BF16) for count in counts + counts[1:]]
            + [pltpu.VMEM((rows, width), BF16)] * 2
            + sems
        )


def line_sum_kernel(count, rows, lag, x_ref, o_ref, come, gone, *sems):
    line = Line(count, rows, lag, x_ref, o_ref, come, gone, sems)
    greet(line.me, count)
    lax.fori_loop(0, line.turns, lambda s, _: (line.turn(s), 0)[1], 0)
    line.finish()


def line_sum(x, cid, rows=16, lag=4):
    count = lax.axis_size("tensor")
    return pl.pallas_call(
        functools.partial(line_sum_kernel, count, rows, lag),
        out_shape=jax.ShapeDtypeStruct(x.shape, BF16),
        in_specs=[pl.BlockSpec(memory_space=pltpu.VMEM)],
        out_specs=pl.BlockSpec(memory_space=pltpu.VMEM),
        scratch_shapes=Line.scratch(x, rows),
        compiler_params=pltpu.CompilerParams(collective_id=cid, has_side_effects=True),
        name="line_sum",
        cost_estimate=pl.CostEstimate(flops=0, bytes_accessed=120_000_000, transcendentals=0),
    )(x)


class Norm:
    def __init__(self, line, layer, wide, trade, refs, outs, bufs):
        self.line, self.layer, self.trade = line, layer, trade
        self.home = refs[:2]
        self.gain, self.ready = refs[2], refs[3] if trade else None
        self.u, self.grad, self.load_sems = bufs[:3]
        bufs = bufs[3:]
        self.mine, self.late = outs[0], outs[-1]
        self.wide = outs[1] if wide else None
        self.got = outs[1] if trade else None
        if trade:
            self.sems = bufs[:2]
            self.small = Small(self.late, self.late, bufs[2:])
        self.section = lax.axis_index("section")
        self.first = 2 * line.lag * (line.count - 1)
        self.rows = 2 * line.rows
        self.steps = self.u.shape[0] // self.rows

    def span(self, index):
        return pl.ds(pl.multiple_of(index * self.rows, self.rows), self.rows)

    def copy(self, source, index):
        return pltpu.make_async_remote_copy(
            src_ref=source.at[self.span(index)],
            dst_ref=self.got.at[self.span(index)],
            send_sem=self.sems[0].at[index],
            recv_sem=self.sems[1].at[index],
            device_id={"section": 1 - self.section},
            device_id_type=MESH,
        )

    def loads(self):
        return [
            pltpu.make_async_copy(self.home[i], (self.u, self.grad)[i], self.load_sems.at[i]) for i in range(2)
        ]

    def start(self):
        for load in self.loads():
            load.start()
        self.late[...] = jnp.zeros_like(self.late)

    def step(self, index):
        span = self.span(index)
        one = self.line.o[span, :].astype(F32)
        _, normed, inverse = norm_forward(self.u[span, :].astype(F32), 1.0, 0.0)
        moved, gain_part, shift_part = norm_backward(one, normed, inverse, self.gain[...])
        moved = self.grad[span, :].astype(F32) + moved
        self.mine[span, :] = moved.astype(BF16)
        if self.wide is not None:
            self.wide[span, :] = moved
        self.late[0:1, :] += gain_part.reshape(1, -1)
        self.late[1:2, :] += shift_part.reshape(1, -1)
        self.late[2:3, :] += jnp.sum(moved.astype(BF16).astype(F32), axis=0, keepdims=True)
        if not self.trade:
            return

        @pl.when(self.section == self.layer)
        def _():
            self.copy(self.ready, index).start()

        @pl.when(self.section != self.layer)
        def _():
            self.copy(self.mine, index).start()

    def finish(self):
        if not self.trade:
            return
        for level in range(self.small.levels + 2):
            self.small.step(level)

        def end_steps(index, _):
            @pl.when(self.section == self.layer)
            def _():
                self.copy(self.ready, index).wait_send()

            @pl.when(self.section != self.layer)
            def _():
                self.copy(self.mine, index).wait_send()

            self.copy(self.got, index).wait_recv()
            return 0

        lax.fori_loop(0, self.steps, end_steps, 0)
        self.small.finish()

    @staticmethod
    def scratch(x, refs, ways, rows):
        loads = [pltpu.VMEM(ref.shape, ref.dtype) for ref in refs[:2]] + [pltpu.SemaphoreType.DMA((2,))]
        if len(refs) == 3:
            return loads
        return loads + Pass.scratch(x, rows) + Small.scratch((8, x.shape[1]), ways)


class Pass:
    def __init__(self, line, pair, got, sems):
        self.pair, self.got, self.sems = pair, got, sems
        self.section = lax.axis_index("section")
        self.rows = 2 * line.rows
        self.steps = got.shape[0] // self.rows

    def copy(self, source, index):
        span = pl.ds(pl.multiple_of(index * self.rows, self.rows), self.rows)
        return pltpu.make_async_remote_copy(
            src_ref=source.at[span],
            dst_ref=self.got.at[span],
            send_sem=self.sems[0].at[index],
            recv_sem=self.sems[1].at[index],
            device_id={"section": 1 - self.section},
            device_id_type=MESH,
        )

    def step(self, index):
        for place in range(2):

            @pl.when(self.section == 1 - place)
            def _():
                self.copy(self.pair[place], index).start()

    def finish(self):
        def end_steps(index, _):
            for place in range(2):

                @pl.when(self.section == 1 - place)
                def _():
                    self.copy(self.pair[place], index).wait_send()

            self.copy(self.got, index).wait_recv()
            return 0

        lax.fori_loop(0, self.steps, end_steps, 0)

    @staticmethod
    def scratch(x, rows):
        return [pltpu.SemaphoreType.DMA((x.shape[0] // (2 * rows),))] * 2


class Small:
    def __init__(self, value, total, bufs):
        self.value, self.total = value, total
        self.levels = lax.axis_size("fsdp").bit_length() - 1
        n = self.levels + 1
        self.away, self.near, self.sems = bufs[:n], bufs[n : 2 * n], bufs[2 * n :]

    def copy(self, level):
        me = lax.axis_index("fsdp")
        if level < self.levels:
            there = {"fsdp": me + (1 - 2 * (me // (1 << level) % 2)) * (1 << level)}
        else:
            there = {"section": 1 - lax.axis_index("section")}
        return pltpu.make_async_remote_copy(
            src_ref=self.away[level],
            dst_ref=self.near[level],
            send_sem=self.sems[0].at[level],
            recv_sem=self.sems[1].at[level],
            device_id=there,
            device_id_type=MESH,
        )

    def step(self, level):
        if level == 0:
            now = self.value[...]
        else:
            self.copy(level - 1).wait_recv()
            now = self.away[level - 1][...] + self.near[level - 1][...]
        if level > self.levels:
            self.total[...] = now
        else:
            self.away[level][...] = now
            self.copy(level).start()

    def finish(self):
        for level in range(self.levels + 1):
            self.copy(level).wait_send()

    @staticmethod
    def scratch(shape, ways):
        n = ways.bit_length()
        return [pltpu.VMEM(shape, F32)] * (2 * n) + [pltpu.SemaphoreType.DMA((n,))] * 2


def line_share_kernel(count, rows, lag, ways, layer, cuts, k, wide, trade, small, passing, *refs):
    refs = list(refs)

    def take(number):
        taken, refs[:] = refs[:number], refs[number:]
        return taken

    x_ref, g_refs = take(1)[0], take(k)
    swap_refs, small_ref, pair = take(3 + trade), take(small), take(2 * passing)
    go_refs = take(k)
    swap_outs, small_out, got = take(2 + wide + trade), take(small), take(passing)
    o_ref = take(1)[0]
    line = Line(count, rows, lag, x_ref, o_ref, *take(2), take(4))
    extra = []
    each = 2 * ways.bit_length() + 2
    swap = Norm(line, layer, wide, trade, swap_refs, swap_outs, take(5 + each if trade else 3))
    swap.start()
    if small:
        sums = Small(small_ref[0], small_out[0], take(each))
        extra.append(sums)
    if passing:
        pass_on = Pass(line, pair, got[0], take(2))
        extra.append(pass_on)
    scratch = refs
    each = len(scratch) // k
    shares = [
        Share(ways, layer, cuts, g_refs[i], go_refs[i], scratch[i * each : (i + 1) * each]) for i in range(k)
    ]
    levels = shares[0].levels
    for share in shares:
        share.load().start()
    greet(line.me, count, shares[0].others())
    for share in shares:
        share.start()
    steps = []
    for level in range(1, levels + 2):
        first, stride = (4, 1) if level == 1 else (3 + 6 * (level - 1), 5)
        steps += [(first + i * cuts * stride, stride, level, share) for i, share in enumerate(shares)]
    steps.append((swap.first, 1, 0, swap))
    turns = max(line.turns, max(first + stride * (cuts - 1) + 1 for first, stride, _, item in steps if item is not swap))

    def turn(s, _):
        line.turn(s)

        @pl.when(s == 3)
        def _():
            for share in shares:
                share.load().wait()

        @pl.when(s == swap.first)
        def _():
            for load in swap.loads():
                load.wait()

        if small:
            for level in range(levels + 2):

                @pl.when(s == 6 * level + 2)
                def _():
                    sums.step(level)

        if passing:

            @pl.when((s % 2 == 0) & (s // 2 < pass_on.steps))
            def _():
                pass_on.step(s // 2)

        for first, stride, level, share in steps:
            past = s - first
            piece = past // stride

            if share is swap:

                @pl.when((past >= 0) & (past < swap.steps))
                def _():
                    swap.step(past)

                continue

            @pl.when((past >= 0) & (past % stride == 0) & (piece < cuts))
            def _():
                share.step(level, piece)
        return 0

    if small:
        turns = max(turns, 6 * (levels + 2) + 1)
    if passing:
        turns = max(turns, 2 * pass_on.steps)
    lax.fori_loop(0, turns, turn, 0)
    swap.finish()
    for item in extra:
        item.finish()
    line.finish()
    for share in shares:
        share.finish()


def line_share(x, grads, layer, cid, norm, wide=False, small=None, pair=(), rows=16, lag=4):
    count, ways = lax.axis_size("tensor"), lax.axis_size("fsdp")
    height = grads[0].shape[0] // ways
    shapes = [(height, g.shape[1]) for g in grads]
    cuts = 3 if height % (3 * TILE) == 0 else 1
    if height % TILE:
        grads = [g.reshape(ways, height, g.shape[1]) for g in grads]
    trade = len(norm) == 4
    total = jax.ShapeDtypeStruct(norm[0].shape, BF16)
    scratch = Line.scratch(x, rows)
    outs = [jax.ShapeDtypeStruct(shape, F32) for shape in shapes]
    args = [x, *grads, *norm]
    outs.append(total)
    if wide:
        outs.append(jax.ShapeDtypeStruct(norm[0].shape, F32))
    if trade:
        outs.append(total)
    outs.append(jax.ShapeDtypeStruct((8, x.shape[1]), F32))
    scratch += Norm.scratch(x, norm, ways, rows)
    if small is not None:
        args.append(small)
        outs.append(jax.ShapeDtypeStruct(small.shape, F32))
        scratch += Small.scratch(small.shape, ways)
    if pair:
        args += pair
        outs.append(total)
        scratch += Pass.scratch(x, rows)
    more = x.shape != norm[0].shape
    if more:
        outs.append(jax.ShapeDtypeStruct(x.shape, BF16))
    else:
        scratch = [pltpu.VMEM(x.shape, BF16)] + scratch
    for g, shape in zip(grads, shapes):
        scratch += Share.scratch(g, shape, ways, cuts)
    vmem = pl.BlockSpec(memory_space=pltpu.VMEM)
    far = pl.BlockSpec(memory_space=pl.ANY)
    ins = [vmem] + [far] * len(grads)
    ins += [far, far, vmem, far] if trade else [far, far, vmem]
    ins += [vmem] if small is not None else []
    ins += [far, far] if pair else []
    spots = [vmem] * len(outs)
    if trade:
        spots[len(grads) + 1] = far
    if pair:
        spots[-1] = far
    return pl.pallas_call(
        functools.partial(
            line_share_kernel,
            count,
            rows,
            lag,
            ways,
            layer,
            cuts,
            len(grads),
            wide,
            trade,
            small is not None,
            bool(pair),
        ),
        out_shape=outs,
        in_specs=ins,
        out_specs=spots,
        scratch_shapes=scratch,
        compiler_params=pltpu.CompilerParams(
            collective_id=cid, has_side_effects=True, vmem_limit_bytes=60 * 1024 * 1024
        ),
        name="line_share",
        cost_estimate=pl.CostEstimate(flops=0, bytes_accessed=120_000_000, transcendentals=0),
    )(*args)


def tensor_sum(value):
    return line_sum(value.astype(BF16), 0).astype(F32)


def gelu_value(value):
    return 0.5 * value * (1.0 + jnp.tanh(GELU_ROOT * (value + GELU_CUBIC * value * value * value)))


def gelu_slope(value):
    inner = jnp.tanh(GELU_ROOT * (value + GELU_CUBIC * value * value * value))
    return 0.5 * (1.0 + inner) + 0.5 * value * (1.0 - inner * inner) * GELU_ROOT * (
        1.0 + 3.0 * GELU_CUBIC * value * value
    )


def norm_forward(token_rows, gain, shift):
    mean_row = jnp.mean(token_rows, axis=-1, keepdims=True)
    centred = token_rows - mean_row
    inverse = lax.rsqrt(jnp.mean(centred * centred, axis=-1, keepdims=True) + NORM_EPS)
    normed = centred * inverse
    return (normed * gain + shift, normed, inverse)


def norm_backward(grad_normed, normed, inverse, gain):
    scaled = grad_normed * gain
    inner = (
        scaled
        - jnp.mean(scaled, axis=-1, keepdims=True)
        - normed * jnp.mean(scaled * normed, axis=-1, keepdims=True)
    )
    return (inverse * inner, jnp.sum(grad_normed * normed, axis=0), jnp.sum(grad_normed, axis=0))


def dot_nn(left, right):
    return jnp.dot(left, right, preferred_element_type=F32)


def dot_nt(left, right):
    return lax.dot_general(left, right, (((1,), (1,)), ((), ())), preferred_element_type=F32)


def dot_tn(left, right):
    return with_layout_constraint(lax.dot_general(left, right, (((0,), (0,)), ((), ())), preferred_element_type=F32), Layout((0,1)))


def layer_forward(inputs, weights, qv_bias, up_bias, gains, shifts, cuts, real, is_last):
    qkv, out_t, up, down_t = weights
    width = qkv.shape[1] // 3
    heads = width // HD
    scale = HD ** (-0.5)
    seq_len = cuts[-1][1]
    normed_one = []
    parts = []
    for part in inputs:
        normed = norm_forward(part.astype(F32), gains[0], shifts[0])[0].astype(BF16)
        normed_one.append(normed)
        parts.append(dot_nn(normed, qkv))
    normed_one = jnp.concatenate(normed_one)
    projected = jnp.concatenate(parts)
    queries = (projected[:, :width] + qv_bias[0]).astype(BF16).reshape(seq_len, heads, HD)
    key_rows = projected[:, width : 2 * width].astype(BF16).reshape(seq_len, heads, HD)
    values = (projected[:, 2 * width :] + qv_bias[1]).astype(BF16).reshape(seq_len, heads, HD)
    context, hidden, normed_two, pre_act, active, outputs, log_total = [], [], [], [], [], [], []
    for (first, last), part in zip(cuts, inputs):
        scores = (
            jnp.einsum("qhd,khd->hqk", queries[first:last], key_rows, preferred_element_type=F32)
            * scale
        )
        scores = jnp.where(lax.broadcasted_iota(jnp.int32, scores.shape, 2) < real, scores, -1e30)
        row_max = jnp.max(scores, axis=-1, keepdims=True)
        exp_scores = jnp.exp(scores - row_max)
        row_total = jnp.sum(exp_scores, axis=-1, keepdims=True)
        probs = (exp_scores / row_total).astype(BF16)
        log_total.append(row_max + jnp.log(row_total))
        mixed = jnp.einsum("hqk,khd->qhd", probs, values, preferred_element_type=F32)
        context.append(mixed.astype(BF16).reshape(last - first, width))
        attn_term = tensor_sum(dot_nt(context[-1], out_t))
        hidden.append(part.astype(F32) + attn_term + shifts[1])
    for rows in hidden:
        normed = norm_forward(rows, gains[1], shifts[2])[0].astype(BF16)
        normed_two.append(normed)
        pre_act.append(dot_nn(normed, up) + up_bias)
        active.append(gelu_value(pre_act[-1]).astype(BF16))
        mlp_term = dot_nt(active[-1], down_t).astype(BF16)
        if is_last:
            outputs.append(None)
            stored_term = mlp_term
            continue
        outputs.append((rows + line_sum(mlp_term, 0).astype(F32) + shifts[3]).astype(BF16))
        stored_term = None
    stored = (
        inputs,
        normed_one,
        queries,
        key_rows,
        values,
        log_total,
        context,
        hidden,
        normed_two,
        pre_act,
        active,
    )
    return outputs, stored, stored_term


def layer_backward(grads, stored, weights, gains, shifts, cuts, real, layer, extra, ready, small):
    qkv, out_t, up, down_t = weights
    (
        inputs,
        normed_one,
        queries,
        key_rows,
        values,
        log_total,
        context,
        hidden,
        normed_two,
        pre_act,
        active,
    ) = stored
    width = qkv.shape[1] // 3
    scale = HD ** (-0.5)
    grad_mix = [part.astype(BF16) for part in grads]
    grad_pre = []
    two_terms = []
    for part, pre in zip(grad_mix, pre_act):
        grad_active = dot_nn(part, down_t)
        grad_pre.append((grad_active * gelu_slope(pre)).astype(BF16))
        two_terms.append(dot_nt(grad_pre[-1], up).astype(BF16))
    mix_all = jnp.concatenate(grad_mix)
    pre_all = jnp.concatenate(grad_pre)
    grad_down = dot_tn(mix_all, jnp.concatenate(active))
    grad_up = dot_tn(jnp.concatenate(normed_two), pre_all)
    count = two_terms[0].shape[0]
    extra_rows, last_shift = hidden[0], shifts[3]
    two = two_terms[0] if extra is None else jnp.concatenate([two_terms[0], extra])
    results = line_share(
        two,
        [grad_down.astype(BF16), grad_up.astype(BF16)],
        layer,
        1 + 2 * layer,
        (hidden[0], grads[0], gains[1:]),
        wide=True,
    )
    grad_down, grad_up, grad_attn, grad_hidden, sums_two = results[:5]
    extra = None if extra is None else results[5][count:]
    up_bias_grad = jnp.sum(pre_all.astype(F32), axis=0)
    mix_shift = jnp.sum(mix_all.astype(F32), axis=0)
    gain_two, shift_two, attn_shift = sums_two[0], sums_two[1], sums_two[2]
    grad_q = []
    grad_k = 0.0
    grad_v = 0.0
    part = grads[0]
    for (first, last), logs in zip(cuts, log_total):
        grad_context = dot_nn(grad_attn, out_t).astype(BF16).reshape(last - first, -1, HD)
        scores = (
            jnp.einsum("qhd,khd->hqk", queries[first:last], key_rows, preferred_element_type=F32)
            * scale
        )
        probs = jnp.exp(scores - logs)
        probs = jnp.where(lax.broadcasted_iota(jnp.int32, scores.shape, 2) < real, probs, 0.0)
        mixed = jnp.einsum("qhd,khd->hqk", grad_context, values, preferred_element_type=F32)
        row_delta = jnp.sum(mixed * probs, axis=-1, keepdims=True)
        grad_scores = (probs * (mixed - row_delta)).astype(BF16)
        grad_v += jnp.einsum("hqk,qhd->khd", probs.astype(BF16), grad_context, preferred_element_type=F32)
        grad_q.append(
            (jnp.einsum("hqk,khd->qhd", grad_scores, key_rows, preferred_element_type=F32) * scale).astype(BF16)
        )
        grad_k += jnp.einsum("hqk,qhd->khd", grad_scores, queries[first:last], preferred_element_type=F32)
    grad_proj = jnp.concatenate(
        [
            jnp.concatenate(grad_q).reshape(-1, width),
            (grad_k * scale).astype(BF16).reshape(-1, width),
            grad_v.astype(BF16).reshape(-1, width),
        ],
        axis=1,
    )
    context_all = jnp.concatenate(context)
    attn_all = grad_attn
    grad_out = dot_tn(attn_all, context_all)
    grad_qkv = dot_tn(normed_one, grad_proj)
    bias_sums = jnp.sum(grad_proj.astype(F32), axis=0)
    send = [dot_nt(grad_proj, qkv).astype(BF16), [grad_qkv.astype(BF16), grad_out.astype(BF16)], layer, 2 + 2 * layer]
    sums = [gain_two, attn_shift, shift_two, mix_shift]
    sums += [bias_sums[:width], bias_sums[2 * width :], up_bias_grad]
    late = other = None
    if ready is not None:
        sums = jnp.concatenate(sums + small)
        sums = jnp.pad(sums, (0, -sums.shape[0] % (8 * part.shape[1]))).reshape(-1, part.shape[1])
        grad_qkv, grad_out, mine, other, late, sums = line_share(
            *send, (inputs[0], grad_hidden, gains[:1], ready), small=sums
        )
    else:
        first = inputs[0]
        last = (extra_rows + extra.astype(F32) + last_shift).astype(BF16)
        norm = (inputs[0], grad_hidden, gains[:1])
        grad_qkv, grad_out, mine, late, other = line_share(*send, norm, pair=(first, last))
        other = (first, last, other)
        sums += [late[0], late[1]]
    return mine, other, (grad_qkv, grad_out, grad_up, grad_down), sums, late


def per_device(
    images,
    cotangent,
    qkv_weight,
    qv_bias,
    out_weight,
    up_weight,
    up_bias,
    down_weight,
    gains,
    shifts,
):
    image_count, seq_len, model_width = images.shape[1:]
    rows_here = qkv_weight.shape[2]
    width = qkv_weight.shape[3]
    units = up_weight.shape[2]
    section = lax.axis_index("section")
    fsdp = lax.axis_index("fsdp")
    is_first = section == 0
    every = ("section", "fsdp")
    padded = -(-seq_len // TILE) * TILE
    cuts = [(0, padded)]

    def gathered(piece):
        whole = lax.all_gather(piece, every, axis=0, tiled=True)
        return whole.reshape(2, -1, piece.shape[1])

    gap = -3 * width % 128
    mixer = gathered(
        jnp.concatenate(
            [
                qkv_weight[0].transpose(1, 0, 2).reshape(rows_here, 3 * width),
                jnp.zeros((rows_here, gap), BF16),
                out_weight[0].T,
            ],
            axis=1,
        )
    )
    qkv = mixer[:, :, : 3 * width]
    out_t = mixer[:, :, 3 * width + gap :]
    up = gathered(up_weight[0])
    down_t = gathered(down_weight[0].T)
    scales = lax.all_gather(
        jnp.concatenate([gains[0], shifts[0]]), every, axis=0, tiled=False
    )
    scales = scales.reshape(2, -1, 6, rows_here).transpose(0, 2, 1, 3).reshape(2, 6, model_width)
    scales = scales.astype(F32)
    biases = lax.all_gather(
        jnp.concatenate([qv_bias.reshape(-1), up_bias.reshape(-1)]), "section", axis=0
    ).astype(F32)

    def padded_rows(array):
        rows = lax.dynamic_index_in_dim(array, section, 0, keepdims=False)[0]
        return jnp.pad(rows, ((0, padded - seq_len), (0, 0)))

    def layer_args(index):
        return (qkv[index], out_t[index], up[index], down_t[index])

    own = padded_rows(images)
    own_grad = padded_rows(cotangent)
    rows = [own[first:last] for first, last in cuts]
    outputs, stored = [], []
    for index in range(2):
        qv = biases[index, : 2 * width].reshape(2, width)
        rows, kept, last_term = layer_forward(
            rows, layer_args(index), qv, biases[index, 2 * width :], scales[index, :2], scales[index, 2:], cuts, seq_len, index == 1
        )
        outputs.append(rows[0])
        stored.append(kept)

    def placed(mine, other):
        mine, other = mine[:seq_len], other[:seq_len]
        return jnp.where(is_first, jnp.stack([mine, other]), jnp.stack([other, mine]))[None, :, None]

    grads = [own_grad[first:last] for first, last in cuts]
    input_grads = [None, None]
    weight_grads = [None, None]
    small = ready = None
    for index in (1, 0):
        mine, other, weight_grads[index], small, late = layer_backward(
            grads,
            stored[index],
            layer_args(index),
            scales[index, :2],
            scales[index, 2:],
            cuts,
            seq_len,
            index,
            last_term if index == 1 else None,
            ready,
            small,
        )
        if index == 1:
            ready, grads = mine, [mine]
            first, last, other = other
            section_outputs = placed(jnp.where(is_first, first, last), other)
        else:
            input_grads = placed(jnp.where(is_first, mine, ready), other)
    grad_qkv, grad_out, grad_up, grad_down = [
        jnp.where(is_first, first, second) for first, second in zip(*weight_grads)
    ]
    each = 4 * model_width + 2 * width + units
    small = small.reshape(-1)
    packed = jnp.where(is_first, small[:each], small[each : 2 * each])
    late = jnp.where(is_first, late[:2], small[2 * each : 2 * each + 2 * model_width].reshape(2, model_width))
    norm_part = packed[: 4 * model_width].reshape(4, model_width)
    norm_part = jnp.stack([late[0], norm_part[0], late[1], norm_part[1], norm_part[2], norm_part[3]])
    norm_part = lax.dynamic_slice_in_dim(norm_part, fsdp * rows_here, rows_here, 1)
    bias_part = packed[4 * model_width :]
    return (
        section_outputs,
        input_grads,
        grad_qkv.reshape(rows_here, 3, width).transpose(1, 0, 2)[None],
        bias_part[: 2 * width].reshape(1, 2, width),
        grad_out.T[None],
        grad_up[None],
        bias_part[2 * width :][None],
        grad_down.T[None],
        norm_part[:2][None],
        norm_part[2:][None],
    )


def solution(mesh):
    return jax.shard_map(
        per_device,
        mesh=mesh,
        in_specs=(
            P(None, "fsdp", None, None),
            P(None, "fsdp", None, None),
            P("section", None, "fsdp", "tensor"),
            P("section", None, "tensor"),
            P("section", "tensor", "fsdp"),
            P("section", "fsdp", "tensor"),
            P("section", "tensor"),
            P("section", "tensor", "fsdp"),
            P("section", None, "fsdp"),
            P("section", None, "fsdp"),
        ),
        out_specs=(
            P("section", None, "fsdp", None, None),
            P("section", None, "fsdp", None, None),
            P("section", None, "fsdp", "tensor"),
            P("section", None, "tensor"),
            P("section", "tensor", "fsdp"),
            P("section", "fsdp", "tensor"),
            P("section", "tensor"),
            P("section", "tensor", "fsdp"),
            P("section", None, "fsdp"),
            P("section", None, "fsdp"),
        ),
        check_vma=False,
    )
```

```python
import functools

import jax
import jax.numpy as jnp
from jax import lax
from jax.experimental import pallas as pl
from jax.experimental.pallas import tpu as pltpu
from jax.sharding import PartitionSpec as P
from jax.experimental.layout import Layout, with_layout_constraint

HD = 72


NORM_EPS = 1e-06
GELU_ROOT = 0.7978845608028654
GELU_CUBIC = 0.044715
F32 = jnp.float32
BF16 = jnp.bfloat16


MESH = pl.DeviceIdType.MESH
TILE = 16


def greet(me, count, others=()):
    barrier = pltpu.get_barrier_semaphore()
    for there, other in ((me > 0, me - 1), (me < count - 1, me + 1)):
        @pl.when(there)
        def _():
            pl.semaphore_signal(barrier, inc=1, device_id={"tensor": other}, device_id_type=MESH)
    for other in others:
        pl.semaphore_signal(barrier, inc=1, device_id=other, device_id_type=MESH)
    peers = (me > 0).astype(jnp.int32) + (me < count - 1).astype(jnp.int32)
    pl.semaphore_wait(barrier, peers + len(others))


class Line:
    def __init__(self, count, rows, lag, x_ref, o_ref, come, gone, sems):
        self.count, self.rows, self.lag = count, rows, lag
        self.x, self.o, self.come, self.gone = x_ref, o_ref, come, gone
        self.red, self.out = sems[:2], sems[2:]
        self.me = lax.axis_index("tensor")
        self.pieces = x_ref.shape[0] // rows
        self.pairs = (self.pieces + 1) // 2
        self.turns = self.pairs + 2 * lag * (count - 1)

    def span(self, piece):
        return pl.ds(pl.multiple_of(piece * self.rows, self.rows), self.rows)

    def send(self, piece, source, target, step, sems):
        return pltpu.make_async_remote_copy(
            src_ref=source.at[self.span(piece)],
            dst_ref=target.at[self.span(piece)],
            send_sem=sems[0].at[piece],
            recv_sem=sems[1].at[piece],
            device_id={"tensor": self.me + step},
            device_id_type=MESH,
        )

    def place(self, step):
        return self.me if step > 0 else self.count - 1 - self.me

    def reduce_step(self, index, step):
        piece = 2 * index + (step < 0)
        ok = (index >= 0) & (piece < self.pieces)
        pos = self.place(step)
        end = self.count - 1
        span = self.span(piece)

        @pl.when(ok & (pos == 0))
        def _():
            self.send(piece, self.x, self.come, step, self.red).start()

        def add():
            self.send(piece, self.come, self.come, step, self.red).wait_recv()
            return (self.x[span, :].astype(F32) + self.come[span, :].astype(F32)).astype(BF16)

        @pl.when(ok & (pos > 0) & (pos < end))
        def _():
            self.gone[span, :] = add()
            self.send(piece, self.gone, self.come, step, self.red).start()

        @pl.when(ok & (pos == end))
        def _():
            self.o[span, :] = add()
            self.send(piece, self.o, self.o, -step, self.out).start()

    def out_step(self, index, step):
        piece = 2 * index + (step < 0)
        ok = (index >= 0) & (piece < self.pieces)
        pos = self.place(step)

        @pl.when(ok & (pos < self.count - 1))
        def _():
            self.send(piece, self.o, self.o, -step, self.out).wait_recv()

        @pl.when(ok & (pos > 0) & (pos < self.count - 1))
        def _():
            self.send(piece, self.o, self.o, -step, self.out).start()

    def turn(self, s):
        for step in (1, -1):
            self.reduce_step(s - self.lag * self.place(step), step)
        back = self.lag * (self.count - 1)
        for step in (1, -1):
            self.out_step(s - back - self.lag * (self.count - 1 - self.place(step)), step)

    def finish(self):
        def end_steps(i, _):
            for step in (1, -1):
                piece = 2 * i + (step < 0)
                pos = self.place(step)

                @pl.when((piece < self.pieces) & (pos < self.count - 1))
                def _():
                    self.send(piece, self.x, self.come, step, self.red).wait_send()

                @pl.when((piece < self.pieces) & (pos > 0))
                def _():
                    self.send(piece, self.o, self.o, -step, self.out).wait_send()
            return 0

        lax.fori_loop(0, self.pairs, end_steps, 0)

    @staticmethod
    def scratch(x, rows):
        return [pltpu.VMEM(x.shape, BF16)] * 2 + [pltpu.SemaphoreType.DMA((x.shape[0] // rows,))] * 4


class Share:
    def __init__(self, ways, layer, cuts, g_ref, o_ref, bufs):
        self.ways, self.layer, self.cuts = ways, layer, cuts
        self.levels = ways.bit_length() - 1
        self.home, self.o = g_ref, o_ref
        self.g, self.load_sem = bufs[:2]
        bufs = bufs[2:]
        n = self.levels
        self.recv, self.stage = bufs[:n], [None] + list(bufs[n : 2 * n - 1])
        bufs = bufs[2 * n - 1 :]
        self.last_recv, self.last_stage = bufs[:2]
        sems = bufs[2:]
        self.sems = [(sems[2 * j], sems[2 * j + 1]) for j in range(n + 1)]
        self.me = lax.axis_index("fsdp")
        self.owner = lax.axis_index("section") == layer
        self.height = o_ref.shape[0]
        self.rows = self.height // cuts

    def others(self):
        return [{"fsdp": self.flip(j)} for j in range(self.levels)] + [
            {"section": 1 - lax.axis_index("section")}
        ]

    def flip(self, level):
        bit = self.me // (1 << level) % 2
        return self.me + (1 - 2 * bit) * (1 << level)

    def blocks(self, level):
        low = self.flip(level) % (1 << (level + 1))
        return [low + (high << (level + 1)) for high in range(self.ways >> (level + 1))]

    def span(self, piece):
        return pl.ds(pl.multiple_of(piece * self.rows, self.rows), self.rows)

    def load(self):
        return pltpu.make_async_copy(self.home, self.g, self.load_sem)

    def own(self, array, block, piece):
        if len(array.shape) == 3:
            return array.at[block, self.span(piece)]
        return array.at[pl.ds(pl.multiple_of(block * self.height + piece * self.rows, self.rows), self.rows)]

    def copy(self, level, block, piece):
        place = block // (1 << (level + 1))
        return pltpu.make_async_remote_copy(
            src_ref=self.own(self.home, block, piece) if level == 0 else self.stage[level].at[place, self.span(piece)],
            dst_ref=self.recv[level].at[place, self.span(piece)],
            send_sem=self.sems[level][0].at[place * self.cuts + piece],
            recv_sem=self.sems[level][1].at[place * self.cuts + piece],
            device_id={"fsdp": self.flip(level)},
            device_id_type=MESH,
        )

    def last_copy(self, piece):
        return pltpu.make_async_remote_copy(
            src_ref=self.last_stage.at[self.span(piece)],
            dst_ref=self.last_recv.at[self.span(piece)],
            send_sem=self.sems[-1][0].at[piece],
            recv_sem=self.sems[-1][1].at[piece],
            device_id={"section": 1 - lax.axis_index("section")},
            device_id_type=MESH,
        )

    def start(self):
        for piece in range(self.cuts):
            for block in self.blocks(0):
                self.copy(0, block, piece).start()

    def total(self, level, block, piece):
        value = self.own(self.g, block, piece)[...].astype(F32)
        for j in range(level):
            self.copy(j, block, piece).wait_recv()
            value += self.recv[j][block // (1 << (j + 1)), self.span(piece), :].astype(F32)
        return value

    def step(self, level, piece):
        if level < self.levels:
            for block in self.blocks(level):
                self.stage[level][block // (1 << (level + 1)), self.span(piece), :] = self.total(
                    level, block, piece
                ).astype(BF16)
                self.copy(level, block, piece).start()
        elif level == self.levels:
            value = self.total(level, self.me, piece)
            self.o[self.span(piece), :] = value

            @pl.when(jnp.logical_not(self.owner))
            def _():
                self.last_stage[self.span(piece), :] = value.astype(BF16)
                self.last_copy(piece).start()
        else:

            @pl.when(self.owner)
            def _():
                self.last_copy(piece).wait_recv()
                self.o[self.span(piece), :] += self.last_recv[self.span(piece), :].astype(F32)

    def finish(self):
        for piece in range(self.cuts):
            for level in range(self.levels):
                for block in self.blocks(level):
                    self.copy(level, block, piece).wait_send()

            @pl.when(jnp.logical_not(self.owner))
            def _():
                self.last_copy(piece).wait_send()

    @staticmethod
    def scratch(g, shape, ways, cuts):
        levels = ways.bit_length() - 1
        rows, width = shape
        counts = [ways >> (j + 1) for j in range(levels)]
        sems = []
        for count in counts + [1]:
            sems += [pltpu.SemaphoreType.DMA((count * cuts,))] * 2
        return (
            [pltpu.VMEM(g.shape, BF16), pltpu.SemaphoreType.DMA]
            + [pltpu.VMEM((count, rows, width), BF16) for count in counts + counts[1:]]
            + [pltpu.VMEM((rows, width), BF16)] * 2
            + sems
        )


def line_sum_kernel(count, rows, lag, ahead, x_ref, o_ref, come, gone, *sems):
    line = Line(count, rows, lag, x_ref, o_ref, come, gone, sems[:4])
    fsdp = lax.axis_index("fsdp")
    odd = fsdp % 2
    greet(line.me, count, [{"fsdp": fsdp + 1 - 2 * odd}] if ahead else [])
    if ahead:

        @pl.when(odd == 1)
        def _():
            pl.semaphore_wait(sems[4], 1)

    def turn(s, _):
        line.turn(s)
        if ahead:

            @pl.when((s == min(ahead, line.turns - 1)) & (odd == 0))
            def _():
                pl.semaphore_signal(sems[4], inc=1, device_id={"fsdp": fsdp + 1}, device_id_type=MESH)
        return 0

    lax.fori_loop(0, line.turns, turn, 0)
    line.finish()


def line_sum(x, cid, ahead=0, rows=16, lag=4):
    count = lax.axis_size("tensor")
    return pl.pallas_call(
        functools.partial(line_sum_kernel, count, rows, lag, ahead),
        out_shape=jax.ShapeDtypeStruct(x.shape, BF16),
        in_specs=[pl.BlockSpec(memory_space=pltpu.VMEM)],
        out_specs=pl.BlockSpec(memory_space=pltpu.VMEM),
        scratch_shapes=Line.scratch(x, rows) + ([pltpu.SemaphoreType.REGULAR] if ahead else []),
        compiler_params=pltpu.CompilerParams(collective_id=cid, has_side_effects=True),
        name="line_sum",
        cost_estimate=pl.CostEstimate(flops=0, bytes_accessed=120_000_000, transcendentals=0),
    )(x)


class Norm:
    def __init__(self, line, layer, wide, trade, refs, outs, bufs):
        self.line, self.layer, self.trade = line, layer, trade
        self.home = refs[:2]
        self.gain, self.ready = refs[2], refs[3] if trade else None
        self.u, self.grad, self.load_sems = bufs[:3]
        bufs = bufs[3:]
        self.mine, self.late = outs[0], outs[-1]
        self.wide = outs[1] if wide else None
        self.got = outs[1] if trade else None
        if trade:
            self.sems = bufs[:2]
            self.small = Small(self.late, self.late, bufs[2:])
        self.section = lax.axis_index("section")
        self.first = 2 * line.lag * (line.count - 1)
        self.rows = 2 * line.rows
        self.steps = self.u.shape[0] // self.rows

    def span(self, index):
        return pl.ds(pl.multiple_of(index * self.rows, self.rows), self.rows)

    def copy(self, source, index):
        return pltpu.make_async_remote_copy(
            src_ref=source.at[self.span(index)],
            dst_ref=self.got.at[self.span(index)],
            send_sem=self.sems[0].at[index],
            recv_sem=self.sems[1].at[index],
            device_id={"section": 1 - self.section},
            device_id_type=MESH,
        )

    def loads(self):
        return [
            pltpu.make_async_copy(self.home[i], (self.u, self.grad)[i], self.load_sems.at[i]) for i in range(2)
        ]

    def start(self):
        for load in self.loads():
            load.start()
        self.late[...] = jnp.zeros_like(self.late)

    def step(self, index):
        span = self.span(index)
        one = self.line.o[span, :].astype(F32)
        _, normed, inverse = norm_forward(self.u[span, :].astype(F32), 1.0, 0.0)
        moved, gain_part, shift_part = norm_backward(one, normed, inverse, self.gain[...])
        moved = self.grad[span, :].astype(F32) + moved
        self.mine[span, :] = moved.astype(BF16)
        if self.wide is not None:
            self.wide[span, :] = moved
        self.late[0:1, :] += gain_part.reshape(1, -1)
        self.late[1:2, :] += shift_part.reshape(1, -1)
        self.late[2:3, :] += jnp.sum(moved.astype(BF16).astype(F32), axis=0, keepdims=True)
        if not self.trade:
            return

        @pl.when(self.section == self.layer)
        def _():
            self.copy(self.ready, index).start()

        @pl.when(self.section != self.layer)
        def _():
            self.copy(self.mine, index).start()

    def finish(self):
        if not self.trade:
            return
        for level in range(self.small.levels + 2):
            self.small.step(level)

        def end_steps(index, _):
            @pl.when(self.section == self.layer)
            def _():
                self.copy(self.ready, index).wait_send()

            @pl.when(self.section != self.layer)
            def _():
                self.copy(self.mine, index).wait_send()

            self.copy(self.got, index).wait_recv()
            return 0

        lax.fori_loop(0, self.steps, end_steps, 0)
        self.small.finish()

    @staticmethod
    def scratch(x, refs, ways, rows):
        loads = [pltpu.VMEM(ref.shape, ref.dtype) for ref in refs[:2]] + [pltpu.SemaphoreType.DMA((2,))]
        if len(refs) == 3:
            return loads
        return loads + Pass.scratch(x, rows) + Small.scratch((8, x.shape[1]), ways)


class Pass:
    def __init__(self, line, pair, got, sems):
        self.pair, self.got, self.sems = pair, got, sems
        self.section = lax.axis_index("section")
        self.rows = 2 * line.rows
        self.steps = got.shape[0] // self.rows

    def copy(self, source, index):
        span = pl.ds(pl.multiple_of(index * self.rows, self.rows), self.rows)
        return pltpu.make_async_remote_copy(
            src_ref=source.at[span],
            dst_ref=self.got.at[span],
            send_sem=self.sems[0].at[index],
            recv_sem=self.sems[1].at[index],
            device_id={"section": 1 - self.section},
            device_id_type=MESH,
        )

    def step(self, index):
        for place in range(2):

            @pl.when(self.section == 1 - place)
            def _():
                self.copy(self.pair[place], index).start()

    def finish(self):
        def end_steps(index, _):
            for place in range(2):

                @pl.when(self.section == 1 - place)
                def _():
                    self.copy(self.pair[place], index).wait_send()

            self.copy(self.got, index).wait_recv()
            return 0

        lax.fori_loop(0, self.steps, end_steps, 0)

    @staticmethod
    def scratch(x, rows):
        return [pltpu.SemaphoreType.DMA((x.shape[0] // (2 * rows),))] * 2


class Small:
    def __init__(self, value, total, bufs):
        self.value, self.total = value, total
        self.levels = lax.axis_size("fsdp").bit_length() - 1
        n = self.levels + 1
        self.away, self.near, self.sems = bufs[:n], bufs[n : 2 * n], bufs[2 * n :]

    def copy(self, level):
        me = lax.axis_index("fsdp")
        if level < self.levels:
            there = {"fsdp": me + (1 - 2 * (me // (1 << level) % 2)) * (1 << level)}
        else:
            there = {"section": 1 - lax.axis_index("section")}
        return pltpu.make_async_remote_copy(
            src_ref=self.away[level],
            dst_ref=self.near[level],
            send_sem=self.sems[0].at[level],
            recv_sem=self.sems[1].at[level],
            device_id=there,
            device_id_type=MESH,
        )

    def step(self, level):
        if level == 0:
            now = self.value[...]
        else:
            self.copy(level - 1).wait_recv()
            now = self.away[level - 1][...] + self.near[level - 1][...]
        if level > self.levels:
            self.total[...] = now
        else:
            self.away[level][...] = now
            self.copy(level).start()

    def finish(self):
        for level in range(self.levels + 1):
            self.copy(level).wait_send()

    @staticmethod
    def scratch(shape, ways):
        n = ways.bit_length()
        return [pltpu.VMEM(shape, F32)] * (2 * n) + [pltpu.SemaphoreType.DMA((n,))] * 2


def line_share_kernel(count, rows, lag, ways, layer, cuts, k, wide, trade, small, passing, *refs):
    refs = list(refs)

    def take(number):
        taken, refs[:] = refs[:number], refs[number:]
        return taken

    x_ref, g_refs = take(1)[0], take(k)
    swap_refs, small_ref, pair = take(3 + trade), take(small), take(2 * passing)
    go_refs = take(k)
    swap_outs, small_out, got = take(2 + wide + trade), take(small), take(passing)
    o_ref = take(1)[0]
    line = Line(count, rows, lag, x_ref, o_ref, *take(2), take(4))
    extra = []
    each = 2 * ways.bit_length() + 2
    swap = Norm(line, layer, wide, trade, swap_refs, swap_outs, take(5 + each if trade else 3))
    swap.start()
    if small:
        sums = Small(small_ref[0], small_out[0], take(each))
        extra.append(sums)
    if passing:
        pass_on = Pass(line, pair, got[0], take(2))
        extra.append(pass_on)
    scratch = refs
    each = len(scratch) // k
    shares = [
        Share(ways, layer, cuts, g_refs[i], go_refs[i], scratch[i * each : (i + 1) * each]) for i in range(k)
    ]
    levels = shares[0].levels
    for share in shares:
        share.load().start()
    greet(line.me, count, shares[0].others())
    for share in shares:
        share.start()
    steps = []
    for level in range(1, levels + 2):
        first, stride = (4, 1) if level == 1 else (3 + 6 * (level - 1), 5)
        steps += [(first + i * cuts * stride, stride, level, share) for i, share in enumerate(shares)]
    steps.append((swap.first, 1, 0, swap))
    turns = max(line.turns, max(first + stride * (cuts - 1) + 1 for first, stride, _, item in steps if item is not swap))

    def turn(s, _):
        line.turn(s)

        @pl.when(s == 3)
        def _():
            for share in shares:
                share.load().wait()

        @pl.when(s == swap.first)
        def _():
            for load in swap.loads():
                load.wait()

        if small:
            for level in range(levels + 2):

                @pl.when(s == 6 * level + 2)
                def _():
                    sums.step(level)

        if passing:

            @pl.when((s % 2 == 0) & (s // 2 < pass_on.steps))
            def _():
                pass_on.step(s // 2)

        for first, stride, level, share in steps:
            past = s - first
            piece = past // stride

            if share is swap:

                @pl.when((past >= 0) & (past < swap.steps))
                def _():
                    swap.step(past)

                continue

            @pl.when((past >= 0) & (past % stride == 0) & (piece < cuts))
            def _():
                share.step(level, piece)
        return 0

    if small:
        turns = max(turns, 6 * (levels + 2) + 1)
    if passing:
        turns = max(turns, 2 * pass_on.steps)
    lax.fori_loop(0, turns, turn, 0)
    swap.finish()
    for item in extra:
        item.finish()
    line.finish()
    for share in shares:
        share.finish()


def line_share(x, grads, layer, cid, norm, wide=False, small=None, pair=(), rows=16, lag=4):
    count, ways = lax.axis_size("tensor"), lax.axis_size("fsdp")
    height = grads[0].shape[0] // ways
    shapes = [(height, g.shape[1]) for g in grads]
    cuts = 3 if height % (3 * TILE) == 0 else 1
    if height % TILE:
        grads = [g.reshape(ways, height, g.shape[1]) for g in grads]
    trade = len(norm) == 4
    total = jax.ShapeDtypeStruct(norm[0].shape, BF16)
    scratch = Line.scratch(x, rows)
    outs = [jax.ShapeDtypeStruct(shape, F32) for shape in shapes]
    args = [x, *grads, *norm]
    outs.append(total)
    if wide:
        outs.append(jax.ShapeDtypeStruct(norm[0].shape, F32))
    if trade:
        outs.append(total)
    outs.append(jax.ShapeDtypeStruct((8, x.shape[1]), F32))
    scratch += Norm.scratch(x, norm, ways, rows)
    if small is not None:
        args.append(small)
        outs.append(jax.ShapeDtypeStruct(small.shape, F32))
        scratch += Small.scratch(small.shape, ways)
    if pair:
        args += pair
        outs.append(total)
        scratch += Pass.scratch(x, rows)
    more = x.shape != norm[0].shape
    if more:
        outs.append(jax.ShapeDtypeStruct(x.shape, BF16))
    else:
        scratch = [pltpu.VMEM(x.shape, BF16)] + scratch
    for g, shape in zip(grads, shapes):
        scratch += Share.scratch(g, shape, ways, cuts)
    vmem = pl.BlockSpec(memory_space=pltpu.VMEM)
    far = pl.BlockSpec(memory_space=pl.ANY)
    ins = [vmem] + [far] * len(grads)
    ins += [far, far, vmem, far] if trade else [far, far, vmem]
    ins += [vmem] if small is not None else []
    ins += [far, far] if pair else []
    spots = [vmem] * len(outs)
    if trade:
        spots[len(grads) + 1] = far
    if pair:
        spots[-1] = far
    return pl.pallas_call(
        functools.partial(
            line_share_kernel,
            count,
            rows,
            lag,
            ways,
            layer,
            cuts,
            len(grads),
            wide,
            trade,
            small is not None,
            bool(pair),
        ),
        out_shape=outs,
        in_specs=ins,
        out_specs=spots,
        scratch_shapes=scratch,
        compiler_params=pltpu.CompilerParams(
            collective_id=cid, has_side_effects=True, vmem_limit_bytes=60 * 1024 * 1024
        ),
        name="line_share",
        cost_estimate=pl.CostEstimate(flops=0, bytes_accessed=120_000_000, transcendentals=0),
    )(*args)


def tensor_sum(value):
    return line_sum(value.astype(BF16), 5).astype(F32)


def gelu_value(value):
    return 0.5 * value * (1.0 + jnp.tanh(GELU_ROOT * (value + GELU_CUBIC * value * value * value)))


def gelu_slope(value):
    inner = jnp.tanh(GELU_ROOT * (value + GELU_CUBIC * value * value * value))
    return 0.5 * (1.0 + inner) + 0.5 * value * (1.0 - inner * inner) * GELU_ROOT * (
        1.0 + 3.0 * GELU_CUBIC * value * value
    )


def norm_forward(token_rows, gain, shift):
    mean_row = jnp.mean(token_rows, axis=-1, keepdims=True)
    centred = token_rows - mean_row
    inverse = lax.rsqrt(jnp.mean(centred * centred, axis=-1, keepdims=True) + NORM_EPS)
    normed = centred * inverse
    return (normed * gain + shift, normed, inverse)


def norm_backward(grad_normed, normed, inverse, gain):
    scaled = grad_normed * gain
    inner = (
        scaled
        - jnp.mean(scaled, axis=-1, keepdims=True)
        - normed * jnp.mean(scaled * normed, axis=-1, keepdims=True)
    )
    return (inverse * inner, jnp.sum(grad_normed * normed, axis=0), jnp.sum(grad_normed, axis=0))


def dot_nn(left, right):
    return jnp.dot(left, right, preferred_element_type=F32)


def dot_nt(left, right):
    return lax.dot_general(left, right, (((1,), (1,)), ((), ())), preferred_element_type=F32)


def dot_tn(left, right):
    return with_layout_constraint(lax.dot_general(left, right, (((0,), (0,)), ((), ())), preferred_element_type=F32), Layout((0,1)))


def layer_forward(inputs, weights, qv_bias, up_bias, gains, shifts, cuts, real, is_last):
    qkv, out_t, up, down_t = weights
    width = qkv.shape[1] // 3
    heads = width // HD
    scale = HD ** (-0.5)
    seq_len = cuts[-1][1]
    normed_one = []
    parts = []
    for part in inputs:
        normed = norm_forward(part.astype(F32), gains[0], shifts[0])[0].astype(BF16)
        normed_one.append(normed)
        parts.append(dot_nn(normed, qkv))
    normed_one = jnp.concatenate(normed_one)
    projected = jnp.concatenate(parts)
    queries = (projected[:, :width] + qv_bias[0]).astype(BF16).reshape(seq_len, heads, HD)
    key_rows = projected[:, width : 2 * width].astype(BF16).reshape(seq_len, heads, HD)
    values = (projected[:, 2 * width :] + qv_bias[1]).astype(BF16).reshape(seq_len, heads, HD)
    context, hidden, normed_two, pre_act, active, outputs, log_total = [], [], [], [], [], [], []
    for (first, last), part in zip(cuts, inputs):
        scores = (
            jnp.einsum("qhd,khd->hqk", queries[first:last], key_rows, preferred_element_type=F32)
            * scale
        )
        scores = jnp.where(lax.broadcasted_iota(jnp.int32, scores.shape, 2) < real, scores, -1e30)
        row_max = jnp.max(scores, axis=-1, keepdims=True)
        exp_scores = jnp.exp(scores - row_max)
        row_total = jnp.sum(exp_scores, axis=-1, keepdims=True)
        probs = (exp_scores / row_total).astype(BF16)
        log_total.append(row_max + jnp.log(row_total))
        mixed = jnp.einsum("hqk,khd->qhd", probs, values, preferred_element_type=F32)
        context.append(mixed.astype(BF16).reshape(last - first, width))
        attn_term = dot_nt(context[-1], out_t).astype(BF16)
        attn_term = (line_sum(attn_term, 5) if is_last else line_sum(attn_term, 0, 46)).astype(F32)
        hidden.append(part.astype(F32) + attn_term + shifts[1])
    for rows in hidden:
        normed = norm_forward(rows, gains[1], shifts[2])[0].astype(BF16)
        normed_two.append(normed)
        pre_act.append(dot_nn(normed, up) + up_bias)
        active.append(gelu_value(pre_act[-1]).astype(BF16))
        mlp_term = dot_nt(active[-1], down_t).astype(BF16)
        if is_last:
            outputs.append(None)
            stored_term = mlp_term
            continue
        outputs.append((rows + line_sum(mlp_term, 5).astype(F32) + shifts[3]).astype(BF16))
        stored_term = None
    stored = (
        inputs,
        normed_one,
        queries,
        key_rows,
        values,
        log_total,
        context,
        hidden,
        normed_two,
        pre_act,
        active,
    )
    return outputs, stored, stored_term


def layer_backward(grads, stored, weights, gains, shifts, cuts, real, layer, extra, ready, small):
    qkv, out_t, up, down_t = weights
    (
        inputs,
        normed_one,
        queries,
        key_rows,
        values,
        log_total,
        context,
        hidden,
        normed_two,
        pre_act,
        active,
    ) = stored
    width = qkv.shape[1] // 3
    scale = HD ** (-0.5)
    grad_mix = [part.astype(BF16) for part in grads]
    grad_pre = []
    two_terms = []
    for part, pre in zip(grad_mix, pre_act):
        grad_active = dot_nn(part, down_t)
        grad_pre.append((grad_active * gelu_slope(pre)).astype(BF16))
        two_terms.append(dot_nt(grad_pre[-1], up).astype(BF16))
    mix_all = jnp.concatenate(grad_mix)
    pre_all = jnp.concatenate(grad_pre)
    grad_down = dot_tn(mix_all, jnp.concatenate(active))
    grad_up = dot_tn(jnp.concatenate(normed_two), pre_all)
    count = two_terms[0].shape[0]
    extra_rows, last_shift = hidden[0], shifts[3]
    two = two_terms[0] if extra is None else jnp.concatenate([two_terms[0], extra])
    results = line_share(
        two,
        [grad_down.astype(BF16), grad_up.astype(BF16)],
        layer,
        1 + 2 * layer,
        (hidden[0], grads[0], gains[1:]),
        wide=True,
    )
    grad_down, grad_up, grad_attn, grad_hidden, sums_two = results[:5]
    extra = None if extra is None else results[5][count:]
    up_bias_grad = jnp.sum(pre_all.astype(F32), axis=0)
    mix_shift = jnp.sum(mix_all.astype(F32), axis=0)
    gain_two, shift_two, attn_shift = sums_two[0], sums_two[1], sums_two[2]
    grad_q = []
    grad_k = 0.0
    grad_v = 0.0
    part = grads[0]
    for (first, last), logs in zip(cuts, log_total):
        grad_context = dot_nn(grad_attn, out_t).astype(BF16).reshape(last - first, -1, HD)
        scores = (
            jnp.einsum("qhd,khd->hqk", queries[first:last], key_rows, preferred_element_type=F32)
            * scale
        )
        probs = jnp.exp(scores - logs)
        probs = jnp.where(lax.broadcasted_iota(jnp.int32, scores.shape, 2) < real, probs, 0.0)
        mixed = jnp.einsum("qhd,khd->hqk", grad_context, values, preferred_element_type=F32)
        row_delta = jnp.sum(mixed * probs, axis=-1, keepdims=True)
        grad_scores = (probs * (mixed - row_delta)).astype(BF16)
        grad_v += jnp.einsum("hqk,qhd->khd", probs.astype(BF16), grad_context, preferred_element_type=F32)
        grad_q.append(
            (jnp.einsum("hqk,khd->qhd", grad_scores, key_rows, preferred_element_type=F32) * scale).astype(BF16)
        )
        grad_k += jnp.einsum("hqk,qhd->khd", grad_scores, queries[first:last], preferred_element_type=F32)
    grad_proj = jnp.concatenate(
        [
            jnp.concatenate(grad_q).reshape(-1, width),
            (grad_k * scale).astype(BF16).reshape(-1, width),
            grad_v.astype(BF16).reshape(-1, width),
        ],
        axis=1,
    )
    context_all = jnp.concatenate(context)
    attn_all = grad_attn
    grad_out = dot_tn(attn_all, context_all)
    grad_qkv = dot_tn(normed_one, grad_proj)
    bias_sums = jnp.sum(grad_proj.astype(F32), axis=0)
    send = [dot_nt(grad_proj, qkv).astype(BF16), [grad_qkv.astype(BF16), grad_out.astype(BF16)], layer, 2 + 2 * layer]
    sums = [gain_two, attn_shift, shift_two, mix_shift]
    sums += [bias_sums[:width], bias_sums[2 * width :], up_bias_grad]
    late = other = None
    if ready is not None:
        sums = jnp.concatenate(sums + small)
        sums = jnp.pad(sums, (0, -sums.shape[0] % (8 * part.shape[1]))).reshape(-1, part.shape[1])
        grad_qkv, grad_out, mine, other, late, sums = line_share(
            *send, (inputs[0], grad_hidden, gains[:1], ready), small=sums
        )
    else:
        first = inputs[0]
        last = (extra_rows + extra.astype(F32) + last_shift).astype(BF16)
        norm = (inputs[0], grad_hidden, gains[:1])
        grad_qkv, grad_out, mine, late, other = line_share(*send, norm, pair=(first, last))
        other = (first, last, other)
        sums += [late[0], late[1]]
    return mine, other, (grad_qkv, grad_out, grad_up, grad_down), sums, late


def per_device(
    images,
    cotangent,
    qkv_weight,
    qv_bias,
    out_weight,
    up_weight,
    up_bias,
    down_weight,
    gains,
    shifts,
):
    image_count, seq_len, model_width = images.shape[1:]
    rows_here = qkv_weight.shape[2]
    width = qkv_weight.shape[3]
    units = up_weight.shape[2]
    section = lax.axis_index("section")
    fsdp = lax.axis_index("fsdp")
    is_first = section == 0
    every = ("section", "fsdp")
    padded = -(-seq_len // TILE) * TILE
    cuts = [(0, padded)]

    def gathered(piece):
        whole = lax.all_gather(piece, every, axis=0, tiled=True)
        return whole.reshape(2, -1, piece.shape[1])

    gap = -3 * width % 128
    mixer = gathered(
        jnp.concatenate(
            [
                qkv_weight[0].transpose(1, 0, 2).reshape(rows_here, 3 * width),
                jnp.zeros((rows_here, gap), BF16),
                out_weight[0].T,
            ],
            axis=1,
        )
    )
    qkv = mixer[:, :, : 3 * width]
    out_t = mixer[:, :, 3 * width + gap :]
    up = gathered(up_weight[0])
    down_t = gathered(down_weight[0].T)
    scales = lax.all_gather(
        jnp.concatenate([gains[0], shifts[0]]), every, axis=0, tiled=False
    )
    scales = scales.reshape(2, -1, 6, rows_here).transpose(0, 2, 1, 3).reshape(2, 6, model_width)
    scales = scales.astype(F32)
    biases = lax.all_gather(
        jnp.concatenate([qv_bias.reshape(-1), up_bias.reshape(-1)]), "section", axis=0
    ).astype(F32)

    def padded_rows(array):
        rows = lax.dynamic_index_in_dim(array, section, 0, keepdims=False)[0]
        return jnp.pad(rows, ((0, padded - seq_len), (0, 0)))

    def layer_args(index):
        return (qkv[index], out_t[index], up[index], down_t[index])

    own = padded_rows(images)
    own_grad = padded_rows(cotangent)
    rows = [own[first:last] for first, last in cuts]
    outputs, stored = [], []
    for index in range(2):
        qv = biases[index, : 2 * width].reshape(2, width)
        rows, kept, last_term = layer_forward(
            rows, layer_args(index), qv, biases[index, 2 * width :], scales[index, :2], scales[index, 2:], cuts, seq_len, index == 1
        )
        outputs.append(rows[0])
        stored.append(kept)

    def placed(mine, other):
        mine, other = mine[:seq_len], other[:seq_len]
        return jnp.where(is_first, jnp.stack([mine, other]), jnp.stack([other, mine]))[None, :, None]

    grads = [own_grad[first:last] for first, last in cuts]
    input_grads = [None, None]
    weight_grads = [None, None]
    small = ready = None
    for index in (1, 0):
        mine, other, weight_grads[index], small, late = layer_backward(
            grads,
            stored[index],
            layer_args(index),
            scales[index, :2],
            scales[index, 2:],
            cuts,
            seq_len,
            index,
            last_term if index == 1 else None,
            ready,
            small,
        )
        if index == 1:
            ready, grads = mine, [mine]
            first, last, other = other
            section_outputs = placed(jnp.where(is_first, first, last), other)
        else:
            input_grads = placed(jnp.where(is_first, mine, ready), other)
    grad_qkv, grad_out, grad_up, grad_down = [
        jnp.where(is_first, first, second) for first, second in zip(*weight_grads)
    ]
    each = 4 * model_width + 2 * width + units
    small = small.reshape(-1)
    packed = jnp.where(is_first, small[:each], small[each : 2 * each])
    late = jnp.where(is_first, late[:2], small[2 * each : 2 * each + 2 * model_width].reshape(2, model_width))
    norm_part = packed[: 4 * model_width].reshape(4, model_width)
    norm_part = jnp.stack([late[0], norm_part[0], late[1], norm_part[1], norm_part[2], norm_part[3]])
    norm_part = lax.dynamic_slice_in_dim(norm_part, fsdp * rows_here, rows_here, 1)
    bias_part = packed[4 * model_width :]
    return (
        section_outputs,
        input_grads,
        grad_qkv.reshape(rows_here, 3, width).transpose(1, 0, 2)[None],
        bias_part[: 2 * width].reshape(1, 2, width),
        grad_out.T[None],
        grad_up[None],
        bias_part[2 * width :][None],
        grad_down.T[None],
        norm_part[:2][None],
        norm_part[2:][None],
    )


def solution(mesh):
    return jax.shard_map(
        per_device,
        mesh=mesh,
        in_specs=(
            P(None, "fsdp", None, None),
            P(None, "fsdp", None, None),
            P("section", None, "fsdp", "tensor"),
            P("section", None, "tensor"),
            P("section", "tensor", "fsdp"),
            P("section", "fsdp", "tensor"),
            P("section", "tensor"),
            P("section", "tensor", "fsdp"),
            P("section", None, "fsdp"),
            P("section", None, "fsdp"),
        ),
        out_specs=(
            P("section", None, "fsdp", None, None),
            P("section", None, "fsdp", None, None),
            P("section", None, "fsdp", "tensor"),
            P("section", None, "tensor"),
            P("section", "tensor", "fsdp"),
            P("section", "fsdp", "tensor"),
            P("section", "tensor"),
            P("section", "tensor", "fsdp"),
            P("section", None, "fsdp"),
            P("section", None, "fsdp"),
        ),
        check_vma=False,
    )
```

```python
import functools

import jax
import jax.numpy as jnp
from jax import lax
from jax.experimental import pallas as pl
from jax.experimental.pallas import tpu as pltpu
from jax.sharding import PartitionSpec as P
from jax.experimental.layout import Layout, with_layout_constraint

HD = 72


NORM_EPS = 1e-06
GELU_ROOT = 0.7978845608028654
GELU_CUBIC = 0.044715
F32 = jnp.float32
BF16 = jnp.bfloat16


MESH = pl.DeviceIdType.MESH
TILE = 16


def greet(me, count, others=()):
    barrier = pltpu.get_barrier_semaphore()
    for there, other in ((me > 0, me - 1), (me < count - 1, me + 1)):
        @pl.when(there)
        def _():
            pl.semaphore_signal(barrier, inc=1, device_id={"tensor": other}, device_id_type=MESH)
    for other in others:
        pl.semaphore_signal(barrier, inc=1, device_id=other, device_id_type=MESH)
    peers = (me > 0).astype(jnp.int32) + (me < count - 1).astype(jnp.int32)
    pl.semaphore_wait(barrier, peers + len(others))


class Line:
    def __init__(self, count, rows, lag, x_ref, o_ref, come, gone, sems):
        self.count, self.rows, self.lag = count, rows, lag
        self.x, self.o, self.come, self.gone = x_ref, o_ref, come, gone
        self.red, self.out = sems[:2], sems[2:]
        self.me = lax.axis_index("tensor")
        self.pieces = x_ref.shape[0] // rows
        self.pairs = (self.pieces + 1) // 2
        self.turns = self.pairs + 2 * lag * (count - 1)

    def span(self, piece):
        return pl.ds(pl.multiple_of(piece * self.rows, self.rows), self.rows)

    def send(self, piece, source, target, step, sems):
        return pltpu.make_async_remote_copy(
            src_ref=source.at[self.span(piece)],
            dst_ref=target.at[self.span(piece)],
            send_sem=sems[0].at[piece],
            recv_sem=sems[1].at[piece],
            device_id={"tensor": self.me + step},
            device_id_type=MESH,
        )

    def place(self, step):
        return self.me if step > 0 else self.count - 1 - self.me

    def reduce_step(self, index, step):
        piece = 2 * index + (step < 0)
        ok = (index >= 0) & (piece < self.pieces)
        pos = self.place(step)
        end = self.count - 1
        span = self.span(piece)

        @pl.when(ok & (pos == 0))
        def _():
            self.send(piece, self.x, self.come, step, self.red).start()

        def add():
            self.send(piece, self.come, self.come, step, self.red).wait_recv()
            return (self.x[span, :].astype(F32) + self.come[span, :].astype(F32)).astype(BF16)

        @pl.when(ok & (pos > 0) & (pos < end))
        def _():
            self.gone[span, :] = add()
            self.send(piece, self.gone, self.come, step, self.red).start()

        @pl.when(ok & (pos == end))
        def _():
            self.o[span, :] = add()
            self.send(piece, self.o, self.o, -step, self.out).start()

    def out_step(self, index, step):
        piece = 2 * index + (step < 0)
        ok = (index >= 0) & (piece < self.pieces)
        pos = self.place(step)

        @pl.when(ok & (pos < self.count - 1))
        def _():
            self.send(piece, self.o, self.o, -step, self.out).wait_recv()

        @pl.when(ok & (pos > 0) & (pos < self.count - 1))
        def _():
            self.send(piece, self.o, self.o, -step, self.out).start()

    def turn(self, s):
        for step in (1, -1):
            self.reduce_step(s - self.lag * self.place(step), step)
        back = self.lag * (self.count - 1)
        for step in (1, -1):
            self.out_step(s - back - self.lag * (self.count - 1 - self.place(step)), step)

    def finish(self):
        def end_steps(i, _):
            for step in (1, -1):
                piece = 2 * i + (step < 0)
                pos = self.place(step)

                @pl.when((piece < self.pieces) & (pos < self.count - 1))
                def _():
                    self.send(piece, self.x, self.come, step, self.red).wait_send()

                @pl.when((piece < self.pieces) & (pos > 0))
                def _():
                    self.send(piece, self.o, self.o, -step, self.out).wait_send()
            return 0

        lax.fori_loop(0, self.pairs, end_steps, 0)

    @staticmethod
    def scratch(x, rows):
        return [pltpu.VMEM(x.shape, BF16)] * 2 + [pltpu.SemaphoreType.DMA((x.shape[0] // rows,))] * 4


class Share:
    def __init__(self, ways, layer, cuts, g_ref, o_ref, bufs):
        self.ways, self.layer, self.cuts = ways, layer, cuts
        self.levels = ways.bit_length() - 1
        self.home, self.o = g_ref, o_ref
        self.g, self.load_sem = bufs[:2]
        bufs = bufs[2:]
        n = self.levels
        self.recv, self.stage = bufs[:n], [None] + list(bufs[n : 2 * n - 1])
        bufs = bufs[2 * n - 1 :]
        self.last_recv, self.last_stage = bufs[:2]
        sems = bufs[2:]
        self.sems = [(sems[2 * j], sems[2 * j + 1]) for j in range(n + 1)]
        self.me = lax.axis_index("fsdp")
        self.owner = lax.axis_index("section") == layer
        self.height = o_ref.shape[0]
        self.rows = self.height // cuts

    def others(self):
        return [{"fsdp": self.flip(j)} for j in range(self.levels)] + [
            {"section": 1 - lax.axis_index("section")}
        ]

    def flip(self, level):
        bit = self.me // (1 << level) % 2
        return self.me + (1 - 2 * bit) * (1 << level)

    def blocks(self, level):
        low = self.flip(level) % (1 << (level + 1))
        return [low + (high << (level + 1)) for high in range(self.ways >> (level + 1))]

    def span(self, piece):
        return pl.ds(pl.multiple_of(piece * self.rows, self.rows), self.rows)

    def load(self):
        return pltpu.make_async_copy(self.home, self.g, self.load_sem)

    def own(self, array, block, piece):
        if len(array.shape) == 3:
            return array.at[block, self.span(piece)]
        return array.at[pl.ds(pl.multiple_of(block * self.height + piece * self.rows, self.rows), self.rows)]

    def copy(self, level, block, piece):
        place = block // (1 << (level + 1))
        return pltpu.make_async_remote_copy(
            src_ref=self.own(self.home, block, piece) if level == 0 else self.stage[level].at[place, self.span(piece)],
            dst_ref=self.recv[level].at[place, self.span(piece)],
            send_sem=self.sems[level][0].at[place * self.cuts + piece],
            recv_sem=self.sems[level][1].at[place * self.cuts + piece],
            device_id={"fsdp": self.flip(level)},
            device_id_type=MESH,
        )

    def last_copy(self, piece):
        return pltpu.make_async_remote_copy(
            src_ref=self.last_stage.at[self.span(piece)],
            dst_ref=self.last_recv.at[self.span(piece)],
            send_sem=self.sems[-1][0].at[piece],
            recv_sem=self.sems[-1][1].at[piece],
            device_id={"section": 1 - lax.axis_index("section")},
            device_id_type=MESH,
        )

    def start(self):
        for piece in range(self.cuts):
            for block in self.blocks(0):
                self.copy(0, block, piece).start()

    def total(self, level, block, piece):
        value = self.own(self.g, block, piece)[...].astype(F32)
        for j in range(level):
            self.copy(j, block, piece).wait_recv()
            value += self.recv[j][block // (1 << (j + 1)), self.span(piece), :].astype(F32)
        return value

    def step(self, level, piece):
        if level < self.levels:
            for block in self.blocks(level):
                self.stage[level][block // (1 << (level + 1)), self.span(piece), :] = self.total(
                    level, block, piece
                ).astype(BF16)
                self.copy(level, block, piece).start()
        elif level == self.levels:
            value = self.total(level, self.me, piece)
            self.o[self.span(piece), :] = value

            @pl.when(jnp.logical_not(self.owner))
            def _():
                self.last_stage[self.span(piece), :] = value.astype(BF16)
                self.last_copy(piece).start()
        else:

            @pl.when(self.owner)
            def _():
                self.last_copy(piece).wait_recv()
                self.o[self.span(piece), :] += self.last_recv[self.span(piece), :].astype(F32)

    def finish(self):
        for piece in range(self.cuts):
            for level in range(self.levels):
                for block in self.blocks(level):
                    self.copy(level, block, piece).wait_send()

            @pl.when(jnp.logical_not(self.owner))
            def _():
                self.last_copy(piece).wait_send()

    @staticmethod
    def scratch(g, shape, ways, cuts):
        levels = ways.bit_length() - 1
        rows, width = shape
        counts = [ways >> (j + 1) for j in range(levels)]
        sems = []
        for count in counts + [1]:
            sems += [pltpu.SemaphoreType.DMA((count * cuts,))] * 2
        return (
            [pltpu.VMEM(g.shape, BF16), pltpu.SemaphoreType.DMA]
            + [pltpu.VMEM((count, rows, width), BF16) for count in counts + counts[1:]]
            + [pltpu.VMEM((rows, width), BF16)] * 2
            + sems
        )


def line_sum_kernel(count, rows, lag, ahead, x_ref, o_ref, come, gone, *sems):
    line = Line(count, rows, lag, x_ref, o_ref, come, gone, sems[:4])
    fsdp = lax.axis_index("fsdp")
    odd = fsdp % 2
    greet(line.me, count, [{"fsdp": fsdp + 1 - 2 * odd}] if ahead else [])
    if ahead:

        @pl.when(odd == 1)
        def _():
            pl.semaphore_wait(sems[4], 1)

    def turn(s, _):
        line.turn(s)
        if ahead:

            @pl.when((s == min(ahead, line.turns - 1)) & (odd == 0))
            def _():
                pl.semaphore_signal(sems[4], inc=1, device_id={"fsdp": fsdp + 1}, device_id_type=MESH)
        return 0

    lax.fori_loop(0, line.turns, turn, 0)
    line.finish()


def line_sum(x, cid, ahead=0, rows=16, lag=4):
    count = lax.axis_size("tensor")
    return pl.pallas_call(
        functools.partial(line_sum_kernel, count, rows, lag, ahead),
        out_shape=jax.ShapeDtypeStruct(x.shape, BF16),
        in_specs=[pl.BlockSpec(memory_space=pltpu.VMEM)],
        out_specs=pl.BlockSpec(memory_space=pltpu.VMEM),
        scratch_shapes=Line.scratch(x, rows) + ([pltpu.SemaphoreType.REGULAR] if ahead else []),
        compiler_params=pltpu.CompilerParams(collective_id=cid, has_side_effects=True),
        name="line_sum",
        cost_estimate=pl.CostEstimate(flops=0, bytes_accessed=120_000_000, transcendentals=0),
    )(x)


class Norm:
    def __init__(self, line, layer, wide, trade, refs, outs, bufs):
        self.line, self.layer, self.trade = line, layer, trade
        self.home = refs[:2]
        self.gain, self.ready = refs[2], refs[3] if trade else None
        self.u, self.grad, self.load_sems = bufs[:3]
        bufs = bufs[3:]
        self.mine, self.late = outs[0], outs[-1]
        self.wide = outs[1] if wide else None
        self.both = outs[0] if trade else None
        if trade:
            self.mine, self.sems = bufs[0], bufs[1:4]
            self.small = Small(self.late, self.late, bufs[4:])
        self.section = lax.axis_index("section")
        self.first = 2 * line.lag * (line.count - 1)
        self.rows = 2 * line.rows
        self.steps = self.u.shape[0] // self.rows

    def span(self, index):
        return pl.ds(pl.multiple_of(index * self.rows, self.rows), self.rows)

    def keep(self, source):
        return pltpu.make_async_copy(source, self.both.at[self.section], self.sems[2].at[0])

    def copy(self, source, index, slot=None):
        return pltpu.make_async_remote_copy(
            src_ref=source.at[self.span(index)],
            dst_ref=self.both.at[self.section if slot is None else slot, self.span(index)],
            send_sem=self.sems[0].at[index],
            recv_sem=self.sems[1].at[index],
            device_id={"section": 1 - self.section},
            device_id_type=MESH,
        )

    def loads(self):
        return [
            pltpu.make_async_copy(self.home[i], (self.u, self.grad)[i], self.load_sems.at[i]) for i in range(2)
        ]

    def start(self):
        for load in self.loads():
            load.start()
        if self.trade:

            @pl.when(self.section != self.layer)
            def _():
                self.keep(self.ready).start()

        self.late[...] = jnp.zeros_like(self.late)

    def step(self, index):
        span = self.span(index)
        one = self.line.o[span, :].astype(F32)
        _, normed, inverse = norm_forward(self.u[span, :].astype(F32), 1.0, 0.0)
        moved, gain_part, shift_part = norm_backward(one, normed, inverse, self.gain[...])
        moved = self.grad[span, :].astype(F32) + moved
        self.mine[span, :] = moved.astype(BF16)
        if self.wide is not None:
            self.wide[span, :] = moved
        self.late[0:1, :] += gain_part.reshape(1, -1)
        self.late[1:2, :] += shift_part.reshape(1, -1)
        self.late[2:3, :] += jnp.sum(moved.astype(BF16).astype(F32), axis=0, keepdims=True)
        if not self.trade:
            return

        @pl.when(self.section == self.layer)
        def _():
            self.copy(self.ready, index).start()

        @pl.when(self.section != self.layer)
        def _():
            self.copy(self.mine, index).start()

    def finish(self):
        if not self.trade:
            return

        @pl.when(self.section == self.layer)
        def _():
            self.keep(self.mine).start()

        for level in range(self.small.levels + 2):
            self.small.step(level)

        def end_steps(index, _):
            @pl.when(self.section == self.layer)
            def _():
                self.copy(self.ready, index).wait_send()

            @pl.when(self.section != self.layer)
            def _():
                self.copy(self.mine, index).wait_send()

            self.copy(self.mine, index, 1 - self.section).wait_recv()
            return 0

        lax.fori_loop(0, self.steps, end_steps, 0)

        @pl.when(self.section == self.layer)
        def _():
            self.keep(self.mine).wait()

        @pl.when(self.section != self.layer)
        def _():
            self.keep(self.ready).wait()

        self.small.finish()

    @staticmethod
    def scratch(x, refs, ways, rows):
        loads = [pltpu.VMEM(ref.shape, ref.dtype) for ref in refs[:2]] + [pltpu.SemaphoreType.DMA((2,))]
        if len(refs) == 3:
            return loads
        return loads + [pltpu.VMEM(refs[0].shape, BF16)] + Pass.scratch(x, rows) + Small.scratch((8, x.shape[1]), ways)


class Pass:
    def __init__(self, line, pair, both, sems):
        self.pair, self.both, self.sems = pair, both, sems
        self.section = lax.axis_index("section")
        self.rows = 2 * line.rows
        self.steps = both.shape[1] // self.rows

    def span(self, index):
        return pl.ds(pl.multiple_of(index * self.rows, self.rows), self.rows)

    def keep(self, source):
        return pltpu.make_async_copy(source, self.both.at[self.section], self.sems[2].at[0])

    def copy(self, source, index, slot=None):
        span = self.span(index)
        return pltpu.make_async_remote_copy(
            src_ref=source.at[span],
            dst_ref=self.both.at[self.section if slot is None else slot, span],
            send_sem=self.sems[0].at[index],
            recv_sem=self.sems[1].at[index],
            device_id={"section": 1 - self.section},
            device_id_type=MESH,
        )

    def start(self):
        for place in range(2):

            @pl.when(self.section == place)
            def _():
                self.keep(self.pair[place]).start()

    def step(self, index):
        for place in range(2):

            @pl.when(self.section == 1 - place)
            def _():
                self.copy(self.pair[place], index).start()

    def finish(self):
        def end_steps(index, _):
            for place in range(2):

                @pl.when(self.section == 1 - place)
                def _():
                    self.copy(self.pair[place], index).wait_send()

            self.copy(self.pair[0], index, 1 - self.section).wait_recv()
            return 0

        lax.fori_loop(0, self.steps, end_steps, 0)
        for place in range(2):

            @pl.when(self.section == place)
            def _():
                self.keep(self.pair[place]).wait()

    @staticmethod
    def scratch(x, rows):
        return [pltpu.SemaphoreType.DMA((x.shape[0] // (2 * rows),))] * 3


class Small:
    def __init__(self, value, total, bufs):
        self.value, self.total = value, total
        self.levels = lax.axis_size("fsdp").bit_length() - 1
        n = self.levels + 1
        self.away, self.near, self.sems = bufs[:n], bufs[n : 2 * n], bufs[2 * n :]

    def copy(self, level):
        me = lax.axis_index("fsdp")
        if level < self.levels:
            there = {"fsdp": me + (1 - 2 * (me // (1 << level) % 2)) * (1 << level)}
        else:
            there = {"section": 1 - lax.axis_index("section")}
        return pltpu.make_async_remote_copy(
            src_ref=self.away[level],
            dst_ref=self.near[level],
            send_sem=self.sems[0].at[level],
            recv_sem=self.sems[1].at[level],
            device_id=there,
            device_id_type=MESH,
        )

    def step(self, level):
        if level == 0:
            now = self.value[...]
        else:
            self.copy(level - 1).wait_recv()
            now = self.away[level - 1][...] + self.near[level - 1][...]
        if level > self.levels:
            self.total[...] = now
        else:
            self.away[level][...] = now
            self.copy(level).start()

    def finish(self):
        for level in range(self.levels + 1):
            self.copy(level).wait_send()

    @staticmethod
    def scratch(shape, ways):
        n = ways.bit_length()
        return [pltpu.VMEM(shape, F32)] * (2 * n) + [pltpu.SemaphoreType.DMA((n,))] * 2


def line_share_kernel(count, rows, lag, ways, layer, cuts, k, wide, trade, small, passing, *refs):
    refs = list(refs)

    def take(number):
        taken, refs[:] = refs[:number], refs[number:]
        return taken

    x_ref, g_refs = take(1)[0], take(k)
    swap_refs, small_ref, pair = take(3 + trade), take(small), take(2 * passing)
    go_refs = take(k)
    swap_outs, small_out, got = take(2 + wide), take(small), take(passing)
    o_ref = take(1)[0]
    line = Line(count, rows, lag, x_ref, o_ref, *take(2), take(4))
    extra = []
    each = 2 * ways.bit_length() + 2
    swap = Norm(line, layer, wide, trade, swap_refs, swap_outs, take(7 + each if trade else 3))
    swap.start()
    if small:
        sums = Small(small_ref[0], small_out[0], take(each))
        extra.append(sums)
    if passing:
        pass_on = Pass(line, pair, got[0], take(3))
        pass_on.start()
        extra.append(pass_on)
    scratch = refs
    each = len(scratch) // k
    shares = [
        Share(ways, layer, cuts, g_refs[i], go_refs[i], scratch[i * each : (i + 1) * each]) for i in range(k)
    ]
    levels = shares[0].levels
    for share in shares:
        share.load().start()
    greet(line.me, count, shares[0].others())
    for share in shares:
        share.start()
    steps = []
    for level in range(1, levels + 2):
        first, stride = (4, 1) if level == 1 else (3 + 6 * (level - 1), 5)
        steps += [(first + i * cuts * stride, stride, level, share) for i, share in enumerate(shares)]
    steps.append((swap.first, 1, 0, swap))
    turns = max(line.turns, max(first + stride * (cuts - 1) + 1 for first, stride, _, item in steps if item is not swap))

    def turn(s, _):
        line.turn(s)

        @pl.when(s == 3)
        def _():
            for share in shares:
                share.load().wait()

        @pl.when(s == swap.first)
        def _():
            for load in swap.loads():
                load.wait()

        if small:
            for level in range(levels + 2):

                @pl.when(s == 6 * level + 2)
                def _():
                    sums.step(level)

        if passing:

            @pl.when((s % 2 == 0) & (s // 2 < pass_on.steps))
            def _():
                pass_on.step(s // 2)

        for first, stride, level, share in steps:
            past = s - first
            piece = past // stride

            if share is swap:

                @pl.when((past >= 0) & (past < swap.steps))
                def _():
                    swap.step(past)

                continue

            @pl.when((past >= 0) & (past % stride == 0) & (piece < cuts))
            def _():
                share.step(level, piece)
        return 0

    if small:
        turns = max(turns, 6 * (levels + 2) + 1)
    if passing:
        turns = max(turns, 2 * pass_on.steps)
    lax.fori_loop(0, turns, turn, 0)
    swap.finish()
    for item in extra:
        item.finish()
    line.finish()
    for share in shares:
        share.finish()


def line_share(x, grads, layer, cid, norm, wide=False, small=None, pair=(), rows=16, lag=4):
    count, ways = lax.axis_size("tensor"), lax.axis_size("fsdp")
    height = grads[0].shape[0] // ways
    shapes = [(height, g.shape[1]) for g in grads]
    cuts = 3 if height % (3 * TILE) == 0 else 1
    if height % TILE:
        grads = [g.reshape(ways, height, g.shape[1]) for g in grads]
    trade = len(norm) == 4
    total = jax.ShapeDtypeStruct(norm[0].shape, BF16)
    scratch = Line.scratch(x, rows)
    outs = [jax.ShapeDtypeStruct(shape, F32) for shape in shapes]
    args = [x, *grads, *norm]
    two = jax.ShapeDtypeStruct((2, *norm[0].shape), BF16)
    outs.append(two if trade else total)
    if wide:
        outs.append(jax.ShapeDtypeStruct(norm[0].shape, F32))
    outs.append(jax.ShapeDtypeStruct((8, x.shape[1]), F32))
    scratch += Norm.scratch(x, norm, ways, rows)
    if small is not None:
        args.append(small)
        outs.append(jax.ShapeDtypeStruct(small.shape, F32))
        scratch += Small.scratch(small.shape, ways)
    if pair:
        args += pair
        outs.append(two)
        scratch += Pass.scratch(x, rows)
    more = x.shape != norm[0].shape
    if more:
        outs.append(jax.ShapeDtypeStruct(x.shape, BF16))
    else:
        scratch = [pltpu.VMEM(x.shape, BF16)] + scratch
    for g, shape in zip(grads, shapes):
        scratch += Share.scratch(g, shape, ways, cuts)
    vmem = pl.BlockSpec(memory_space=pltpu.VMEM)
    far = pl.BlockSpec(memory_space=pl.ANY)
    ins = [vmem] + [far] * len(grads)
    ins += [far, far, vmem, far] if trade else [far, far, vmem]
    ins += [vmem] if small is not None else []
    ins += [far, far] if pair else []
    spots = [vmem] * len(outs)
    if trade:
        spots[len(grads)] = far
    if pair:
        spots[-1] = far
    return pl.pallas_call(
        functools.partial(
            line_share_kernel,
            count,
            rows,
            lag,
            ways,
            layer,
            cuts,
            len(grads),
            wide,
            trade,
            small is not None,
            bool(pair),
        ),
        out_shape=outs,
        in_specs=ins,
        out_specs=spots,
        scratch_shapes=scratch,
        compiler_params=pltpu.CompilerParams(
            collective_id=cid, has_side_effects=True, vmem_limit_bytes=60 * 1024 * 1024
        ),
        name="line_share",
        cost_estimate=pl.CostEstimate(flops=0, bytes_accessed=120_000_000, transcendentals=0),
    )(*args)


def tensor_sum(value):
    return line_sum(value.astype(BF16), 5).astype(F32)


def gelu_value(value):
    return 0.5 * value * (1.0 + jnp.tanh(GELU_ROOT * (value + GELU_CUBIC * value * value * value)))


def gelu_slope(value):
    inner = jnp.tanh(GELU_ROOT * (value + GELU_CUBIC * value * value * value))
    return 0.5 * (1.0 + inner) + 0.5 * value * (1.0 - inner * inner) * GELU_ROOT * (
        1.0 + 3.0 * GELU_CUBIC * value * value
    )


def norm_forward(token_rows, gain, shift):
    mean_row = jnp.mean(token_rows, axis=-1, keepdims=True)
    centred = token_rows - mean_row
    inverse = lax.rsqrt(jnp.mean(centred * centred, axis=-1, keepdims=True) + NORM_EPS)
    normed = centred * inverse
    return (normed * gain + shift, normed, inverse)


def norm_backward(grad_normed, normed, inverse, gain):
    scaled = grad_normed * gain
    inner = (
        scaled
        - jnp.mean(scaled, axis=-1, keepdims=True)
        - normed * jnp.mean(scaled * normed, axis=-1, keepdims=True)
    )
    return (inverse * inner, jnp.sum(grad_normed * normed, axis=0), jnp.sum(grad_normed, axis=0))


def dot_nn(left, right):
    return jnp.dot(left, right, preferred_element_type=F32)


def dot_nt(left, right):
    return lax.dot_general(left, right, (((1,), (1,)), ((), ())), preferred_element_type=F32)


def dot_tn(left, right):
    return with_layout_constraint(lax.dot_general(left, right, (((0,), (0,)), ((), ())), preferred_element_type=F32), Layout((0,1)))


def layer_forward(inputs, weights, qv_bias, up_bias, gains, shifts, cuts, real, is_last):
    qkv, out_t, up, down_t = weights
    width = qkv.shape[1] // 3
    heads = width // HD
    scale = HD ** (-0.5)
    seq_len = cuts[-1][1]
    normed_one = []
    parts = []
    for part in inputs:
        normed = norm_forward(part.astype(F32), gains[0], shifts[0])[0].astype(BF16)
        normed_one.append(normed)
        parts.append(dot_nn(normed, qkv))
    normed_one = jnp.concatenate(normed_one)
    projected = jnp.concatenate(parts)
    queries = (projected[:, :width] + qv_bias[0]).astype(BF16).reshape(seq_len, heads, HD)
    key_rows = projected[:, width : 2 * width].astype(BF16).reshape(seq_len, heads, HD)
    values = (projected[:, 2 * width :] + qv_bias[1]).astype(BF16).reshape(seq_len, heads, HD)
    context, hidden, normed_two, pre_act, active, outputs, log_total = [], [], [], [], [], [], []
    for (first, last), part in zip(cuts, inputs):
        scores = (
            jnp.einsum("qhd,khd->hqk", queries[first:last], key_rows, preferred_element_type=F32)
            * scale
        )
        scores = jnp.where(lax.broadcasted_iota(jnp.int32, scores.shape, 2) < real, scores, -1e30)
        row_max = jnp.max(scores, axis=-1, keepdims=True)
        exp_scores = jnp.exp(scores - row_max)
        row_total = jnp.sum(exp_scores, axis=-1, keepdims=True)
        probs = (exp_scores / row_total).astype(BF16)
        log_total.append(row_max + jnp.log(row_total))
        mixed = jnp.einsum("hqk,khd->qhd", probs, values, preferred_element_type=F32)
        context.append(mixed.astype(BF16).reshape(last - first, width))
        attn_term = dot_nt(context[-1], out_t).astype(BF16)
        attn_term = (line_sum(attn_term, 5) if is_last else line_sum(attn_term, 0, 46)).astype(F32)
        hidden.append(part.astype(F32) + attn_term + shifts[1])
    for rows in hidden:
        normed = norm_forward(rows, gains[1], shifts[2])[0].astype(BF16)
        normed_two.append(normed)
        pre_act.append(dot_nn(normed, up) + up_bias)
        active.append(gelu_value(pre_act[-1]).astype(BF16))
        mlp_term = dot_nt(active[-1], down_t).astype(BF16)
        if is_last:
            outputs.append(None)
            stored_term = mlp_term
            continue
        outputs.append((rows + line_sum(mlp_term, 5).astype(F32) + shifts[3]).astype(BF16))
        stored_term = None
    stored = (
        inputs,
        normed_one,
        queries,
        key_rows,
        values,
        log_total,
        context,
        hidden,
        normed_two,
        pre_act,
        active,
    )
    return outputs, stored, stored_term


def layer_backward(grads, stored, weights, gains, shifts, cuts, real, layer, extra, ready, small):
    qkv, out_t, up, down_t = weights
    (
        inputs,
        normed_one,
        queries,
        key_rows,
        values,
        log_total,
        context,
        hidden,
        normed_two,
        pre_act,
        active,
    ) = stored
    width = qkv.shape[1] // 3
    scale = HD ** (-0.5)
    grad_mix = [part.astype(BF16) for part in grads]
    grad_pre = []
    two_terms = []
    for part, pre in zip(grad_mix, pre_act):
        grad_active = dot_nn(part, down_t)
        grad_pre.append((grad_active * gelu_slope(pre)).astype(BF16))
        two_terms.append(dot_nt(grad_pre[-1], up).astype(BF16))
    mix_all = jnp.concatenate(grad_mix)
    pre_all = jnp.concatenate(grad_pre)
    grad_down = dot_tn(mix_all, jnp.concatenate(active))
    grad_up = dot_tn(jnp.concatenate(normed_two), pre_all)
    count = two_terms[0].shape[0]
    extra_rows, last_shift = hidden[0], shifts[3]
    two = two_terms[0] if extra is None else jnp.concatenate([two_terms[0], extra])
    results = line_share(
        two,
        [grad_down.astype(BF16), grad_up.astype(BF16)],
        layer,
        1 + 2 * layer,
        (hidden[0], grads[0], gains[1:]),
        wide=True,
    )
    grad_down, grad_up, grad_attn, grad_hidden, sums_two = results[:5]
    extra = None if extra is None else results[5][count:]
    up_bias_grad = jnp.sum(pre_all.astype(F32), axis=0)
    mix_shift = jnp.sum(mix_all.astype(F32), axis=0)
    gain_two, shift_two, attn_shift = sums_two[0], sums_two[1], sums_two[2]
    grad_q = []
    grad_k = 0.0
    grad_v = 0.0
    part = grads[0]
    for (first, last), logs in zip(cuts, log_total):
        grad_context = dot_nn(grad_attn, out_t).astype(BF16).reshape(last - first, -1, HD)
        scores = (
            jnp.einsum("qhd,khd->hqk", queries[first:last], key_rows, preferred_element_type=F32)
            * scale
        )
        probs = jnp.exp(scores - logs)
        probs = jnp.where(lax.broadcasted_iota(jnp.int32, scores.shape, 2) < real, probs, 0.0)
        mixed = jnp.einsum("qhd,khd->hqk", grad_context, values, preferred_element_type=F32)
        row_delta = jnp.sum(mixed * probs, axis=-1, keepdims=True)
        grad_scores = (probs * (mixed - row_delta)).astype(BF16)
        grad_v += jnp.einsum("hqk,qhd->khd", probs.astype(BF16), grad_context, preferred_element_type=F32)
        grad_q.append(
            (jnp.einsum("hqk,khd->qhd", grad_scores, key_rows, preferred_element_type=F32) * scale).astype(BF16)
        )
        grad_k += jnp.einsum("hqk,qhd->khd", grad_scores, queries[first:last], preferred_element_type=F32)
    grad_proj = jnp.concatenate(
        [
            jnp.concatenate(grad_q).reshape(-1, width),
            (grad_k * scale).astype(BF16).reshape(-1, width),
            grad_v.astype(BF16).reshape(-1, width),
        ],
        axis=1,
    )
    context_all = jnp.concatenate(context)
    attn_all = grad_attn
    grad_out = dot_tn(attn_all, context_all)
    grad_qkv = dot_tn(normed_one, grad_proj)
    bias_sums = jnp.sum(grad_proj.astype(F32), axis=0)
    send = [dot_nt(grad_proj, qkv).astype(BF16), [grad_qkv.astype(BF16), grad_out.astype(BF16)], layer, 2 + 2 * layer]
    sums = [gain_two, attn_shift, shift_two, mix_shift]
    sums += [bias_sums[:width], bias_sums[2 * width :], up_bias_grad]
    late = other = None
    if ready is not None:
        sums = jnp.concatenate(sums + small)
        sums = jnp.pad(sums, (0, -sums.shape[0] % (8 * part.shape[1]))).reshape(-1, part.shape[1])
        mine = None
        grad_qkv, grad_out, other, late, sums = line_share(
            *send, (inputs[0], grad_hidden, gains[:1], ready), small=sums
        )
    else:
        first = inputs[0]
        last = (extra_rows + extra.astype(F32) + last_shift).astype(BF16)
        norm = (inputs[0], grad_hidden, gains[:1])
        grad_qkv, grad_out, mine, late, other = line_share(*send, norm, pair=(first, last))
        sums += [late[0], late[1]]
    return mine, other, (grad_qkv, grad_out, grad_up, grad_down), sums, late


def per_device(
    images,
    cotangent,
    qkv_weight,
    qv_bias,
    out_weight,
    up_weight,
    up_bias,
    down_weight,
    gains,
    shifts,
):
    image_count, seq_len, model_width = images.shape[1:]
    rows_here = qkv_weight.shape[2]
    width = qkv_weight.shape[3]
    units = up_weight.shape[2]
    section = lax.axis_index("section")
    fsdp = lax.axis_index("fsdp")
    is_first = section == 0
    every = ("section", "fsdp")
    padded = -(-seq_len // TILE) * TILE
    cuts = [(0, padded)]

    def gathered(piece):
        whole = lax.all_gather(piece, every, axis=0, tiled=True)
        return whole.reshape(2, -1, piece.shape[1])

    gap = -3 * width % 128
    mixer = gathered(
        jnp.concatenate(
            [
                qkv_weight[0].transpose(1, 0, 2).reshape(rows_here, 3 * width),
                jnp.zeros((rows_here, gap), BF16),
                out_weight[0].T,
            ],
            axis=1,
        )
    )
    qkv = mixer[:, :, : 3 * width]
    out_t = mixer[:, :, 3 * width + gap :]
    up = gathered(up_weight[0])
    down_t = gathered(down_weight[0].T)
    scales = lax.all_gather(
        jnp.concatenate([gains[0], shifts[0]]), every, axis=0, tiled=False
    )
    scales = scales.reshape(2, -1, 6, rows_here).transpose(0, 2, 1, 3).reshape(2, 6, model_width)
    scales = scales.astype(F32)
    biases = lax.all_gather(
        jnp.concatenate([qv_bias.reshape(-1), up_bias.reshape(-1)]), "section", axis=0
    ).astype(F32)

    def padded_rows(array):
        rows = lax.dynamic_index_in_dim(array, section, 0, keepdims=False)[0]
        return jnp.pad(rows, ((0, padded - seq_len), (0, 0)))

    def layer_args(index):
        return (qkv[index], out_t[index], up[index], down_t[index])

    own = padded_rows(images)
    own_grad = padded_rows(cotangent)
    rows = [own[first:last] for first, last in cuts]
    outputs, stored = [], []
    for index in range(2):
        qv = biases[index, : 2 * width].reshape(2, width)
        rows, kept, last_term = layer_forward(
            rows, layer_args(index), qv, biases[index, 2 * width :], scales[index, :2], scales[index, 2:], cuts, seq_len, index == 1
        )
        outputs.append(rows[0])
        stored.append(kept)

    def placed(both):
        return both[None, :, None, :seq_len]

    grads = [own_grad[first:last] for first, last in cuts]
    input_grads = [None, None]
    weight_grads = [None, None]
    small = ready = None
    for index in (1, 0):
        mine, other, weight_grads[index], small, late = layer_backward(
            grads,
            stored[index],
            layer_args(index),
            scales[index, :2],
            scales[index, 2:],
            cuts,
            seq_len,
            index,
            last_term if index == 1 else None,
            ready,
            small,
        )
        if index == 1:
            ready, grads = mine, [mine]
            section_outputs = placed(other)
        else:
            input_grads = placed(other)
    grad_qkv, grad_out, grad_up, grad_down = [
        jnp.where(is_first, first, second) for first, second in zip(*weight_grads)
    ]
    each = 4 * model_width + 2 * width + units
    small = small.reshape(-1)
    packed = jnp.where(is_first, small[:each], small[each : 2 * each])
    late = jnp.where(is_first, late[:2], small[2 * each : 2 * each + 2 * model_width].reshape(2, model_width))
    norm_part = packed[: 4 * model_width].reshape(4, model_width)
    norm_part = jnp.stack([late[0], norm_part[0], late[1], norm_part[1], norm_part[2], norm_part[3]])
    norm_part = lax.dynamic_slice_in_dim(norm_part, fsdp * rows_here, rows_here, 1)
    bias_part = packed[4 * model_width :]
    return (
        section_outputs,
        input_grads,
        grad_qkv.reshape(rows_here, 3, width).transpose(1, 0, 2)[None],
        bias_part[: 2 * width].reshape(1, 2, width),
        grad_out.T[None],
        grad_up[None],
        bias_part[2 * width :][None],
        grad_down.T[None],
        norm_part[:2][None],
        norm_part[2:][None],
    )


def solution(mesh):
    return jax.shard_map(
        per_device,
        mesh=mesh,
        in_specs=(
            P(None, "fsdp", None, None),
            P(None, "fsdp", None, None),
            P("section", None, "fsdp", "tensor"),
            P("section", None, "tensor"),
            P("section", "tensor", "fsdp"),
            P("section", "fsdp", "tensor"),
            P("section", "tensor"),
            P("section", "tensor", "fsdp"),
            P("section", None, "fsdp"),
            P("section", None, "fsdp"),
        ),
        out_specs=(
            P("section", None, "fsdp", None, None),
            P("section", None, "fsdp", None, None),
            P("section", None, "fsdp", "tensor"),
            P("section", None, "tensor"),
            P("section", "tensor", "fsdp"),
            P("section", "fsdp", "tensor"),
            P("section", "tensor"),
            P("section", "tensor", "fsdp"),
            P("section", None, "fsdp"),
            P("section", None, "fsdp"),
        ),
        check_vma=False,
    )
```
